512 devices in a mesh: row: 16 (over z), wide: 32 (over x, y, core).
Axes of the slice: x: 4, y: 4, z: 16, core: 2. Of those that a mesh axis runs over, the one named last changes fastest.
Arguments:
- eigvec_t: float32 [2048, 32768], P(('row', 'wide')), may hold values from -6 to 6
- householder: float32 [64, 32, 32768], P('row', None, 'wide'), may hold values from -0.0625 to 0.0625
- wy_factor: float32 [6, 32, 32], replicated, may hold values from -0.5 to 0.5, as said below
- block_place: int32 [6], replicated, may hold values from 0 to 63, as said below
- offsets: int32 [6], replicated, may hold values from 0 to 16383, as said below
Outputs:
- vectors: float32 [2048, 32768], P('row', 'wide')
The draws below stay inside these ranges and needn't reach their ends.
Inputs may be any that keep to these rules, and one draw needn't show every extreme that they name: wy_factor[s] is upper triangular. `offsets`: some step has offset 0 and some step has offset 32768 // 2 - 1. `block_place`: no stack position appears twice; positions 0 and 63 both appear.
All inputs are finite; a program needn't handle non-finite values.
Results may differ from the reference program's by a relative error of at most 0.0003.
Values sent between devices are 32-bit elements; how exact they have to be, the bound alone decides.
A program may use at most 64 MiB of HBM per device.

```python
import jax
import jax.numpy as jnp
from jax import lax

N = 32768
BW = 32
K = 2048
STACK = 64
STEPS = 6


def draw_wy_factor(key, part):
    key_diag, key_off = jax.random.split(jax.random.fold_in(key, 7))
    diag = jax.random.uniform(key_diag, (STEPS, BW), jnp.float32, 0.15, 0.35)
    upper = jnp.clip(0.06 * jax.random.normal(key_off, (STEPS, BW, BW), jnp.float32), -0.3, 0.3)
    upper = jnp.triu(upper, 1)
    return upper + diag[:, :, None] * jnp.eye(BW, dtype=jnp.float32)[None, :, :]


def draw_block_place(key, part):
    key_pick, key_order = jax.random.split(jax.random.fold_in(key, 13))
    inner = 1 + jax.random.permutation(key_pick, jnp.arange(STACK - 2, dtype=jnp.int32))
    chosen = jnp.concatenate([jnp.array([0, STACK - 1], dtype=jnp.int32), inner.astype(jnp.int32)])[:STEPS]
    return jax.random.permutation(key_order, chosen).astype(jnp.int32)


def draw_offsets(key, part):
    key_vals, key_perm = jax.random.split(jax.random.fold_in(key, 11))
    values = jax.random.randint(key_vals, (STEPS,), 0, N // 2, jnp.int32)
    order = jax.random.permutation(key_perm, STEPS)
    values = values.at[order[0]].set(0)
    values = values.at[order[1]].set(N // 2 - 1)
    return values.astype(jnp.int32)


def levels(rng, extent, pieces, smallest, top_value):
    loudness, own = 1.0, jax.random.fold_in(rng, 6)
    for dim, parts in pieces:
        draws = jnp.exp(jax.random.uniform(jax.random.fold_in(own, dim), (parts,), jnp.float32, smallest / len(pieces), top_value / len(pieces)))
        loudness = loudness * jnp.repeat(draws, extent[dim] // parts).reshape([-1 if axis == dim else 1 for axis in range(len(extent))])
    return loudness


def gaussian(own_key, dims, width, limit, shards=(), held_as=jnp.bfloat16):
    level = levels(own_key, dims, shards, -0.22, 0.18) if shards else 1.0
    drawn = jax.random.normal(own_key, dims, jnp.float32) * width * level
    return jnp.minimum(jnp.maximum(drawn, -limit), limit).astype(held_as)


def setup_inputs(seed: int = 0) -> dict:
    key_of = jax.random.split(jax.random.key(seed), 6)
    return {
        "eigvec_t": gaussian(key_of[0], (K, N), 1.0, 6.0, ((0, 512),), jnp.float32),
        "householder": gaussian(key_of[1], (STACK, BW, N), (N // 4) ** -0.5, 0.0625, ((0, 16), (2, 32)), jnp.float32),
        "wy_factor": draw_wy_factor(jax.random.fold_in(key_of[5], 71), 0),
        "block_place": draw_block_place(jax.random.fold_in(key_of[5], 71), 0),
        "offsets": draw_offsets(jax.random.fold_in(key_of[5], 71), 0),
    }


def reference(eigvec_t, householder, wy_factor, block_place, offsets):
    highest = lax.Precision.HIGHEST
    columns = jnp.arange(N, dtype=jnp.int32)

    def apply_step(current, s):
        place = block_place[s].astype(jnp.int32)
        vecs = lax.dynamic_index_in_dim(householder, place, 0, keepdims=False)
        vecs = jnp.where(columns[None, :] >= offsets[s], vecs, jnp.zeros_like(vecs))
        factor = lax.dynamic_index_in_dim(wy_factor, s, 0, keepdims=False)
        inner = jnp.dot(current, vecs.T, precision=highest)
        scaled = jnp.dot(inner, factor.T, precision=highest)
        return current - jnp.dot(scaled, vecs, precision=highest), None

    result, unused = lax.scan(apply_step, eigvec_t, jnp.arange(STEPS, dtype=jnp.int32))
    return result
```

```python
import jax
import jax.numpy as jnp
from jax import lax
from jax.sharding import PartitionSpec as P

HIGHEST = lax.Precision.HIGHEST


def body(eigvec_t, householder, wy_factor, block_place, offsets):
    current = lax.all_to_all(eigvec_t, "wide", split_axis=1, concat_axis=0, tiled=True)
    slots, width, ncols = householder.shape
    steps = block_place.shape[0]
    rows = current.shape[0]
    columns = lax.axis_index("wide") * ncols + jnp.arange(ncols, dtype=jnp.int32)

    stored = jnp.take(householder, block_place % slots, axis=0)
    mine = (block_place // slots == lax.axis_index("row"))[:, None, None]
    keep = mine & (columns[None, None, :] >= offsets[:, None, None])
    vecs = lax.psum(jnp.where(keep, stored, 0.0), "row")
    vecs = vecs.reshape(steps * width, ncols)

    left = jnp.concatenate([current, vecs], axis=0)
    products = lax.psum(jnp.dot(left, vecs.T, precision=HIGHEST), "wide")
    inner, gram = products[:rows], products[rows:]

    scaled = []
    for s in range(steps):
        at = slice(s * width, (s + 1) * width)
        w = inner[:, at]
        if s:
            w = w - jnp.dot(jnp.concatenate(scaled, axis=1), gram[: s * width, at], precision=HIGHEST)
        scaled.append(jnp.dot(w, wy_factor[s].T, precision=HIGHEST))
    return current - jnp.dot(jnp.concatenate(scaled, axis=1), vecs, precision=HIGHEST)


def solution(mesh):
    return jax.shard_map(
        body,
        mesh=mesh,
        in_specs=(P(("row", "wide"), None), P("row", None, "wide"), P(), P(), P()),
        out_specs=P("row", "wide"),
        check_vma=False,
    )
```

```python
import functools

import jax
import jax.numpy as jnp
from jax import lax
from jax.experimental import pallas as pl
from jax.experimental.pallas import tpu as pltpu
from jax.sharding import PartitionSpec as P

HIGHEST = lax.Precision.HIGHEST
MESH = pl.DeviceIdType.MESH
STEPS, BW, SLAB = 6, 32, 128
GRAM_TILES = [(i, 0) for i in range(12)] + [(i, 1) for i in range(20)]


def dot_t(a, b):
    return lax.dot_general(a, b, (((1,), (1,)), ((), ())), precision=HIGHEST, preferred_element_type=jnp.float32)


def dot(a, b):
    return jnp.dot(a, b, precision=HIGHEST, preferred_element_type=jnp.float32)


def kernel(n_row, n_wide, place_ref, offset_ref, x_ref, h_ref, t_ref, out_ref,
           own, right_buf, left_buf, xs, vs, part, gather_in, total, gathered,
           right_sem, left_sem, x_sem, red_sem, all_sem, send_sem, local_sem):
    r = lax.axis_index("row")
    w = lax.axis_index("wide")
    slots = h_ref.shape[0]
    slabs = h_ref.shape[2] // SLAB
    per = slabs * STEPS // n_row
    right = lax.rem(r + 1, n_row)
    left = lax.rem(r + n_row - 1, n_row)

    barrier = pltpu.get_barrier_semaphore()
    pl.semaphore_signal(barrier, inc=1, device_id={"row": right}, device_id_type=MESH)
    pl.semaphore_signal(barrier, inc=1, device_id={"row": left}, device_id_type=MESH)

    def greet(d, carry):
        peer = lax.rem(w + d, n_wide)
        pl.semaphore_signal(barrier, inc=1, device_id={"wide": peer}, device_id_type=MESH)
        return carry

    lax.fori_loop(1, n_wide, greet, 0)

    lane = lax.broadcasted_iota(jnp.int32, (BW, SLAB), 1) + w * (slabs * SLAB)
    for s in range(STEPS):
        place = place_ref[s]
        start = jnp.where(lax.div(place, slots) == r, offset_ref[s], n_wide * slabs * SLAB)
        slot = lax.rem(place, slots)
        for k in range(slabs):
            block = h_ref[slot, :, k * SLAB:(k + 1) * SLAB]
            own[k * STEPS + s] = jnp.where(lane + k * SLAB >= start, block, 0.0)

    mine = pltpu.make_async_copy(x_ref.at[w], xs.at[:, w], local_sem)
    mine.start()
    pl.semaphore_wait(barrier, n_wide + 1)

    def send_x(d):
        peer = lax.rem(w + d, n_wide)
        pltpu.make_async_remote_copy(
            src_ref=x_ref.at[peer], dst_ref=xs.at[:, w], send_sem=send_sem.at[2], recv_sem=x_sem,
            device_id={"wide": peer}, device_id_type=MESH).start()

    def hop(buf, c, sems, send, t, j, to):
        return pltpu.make_async_remote_copy(
            src_ref=buf.at[c], dst_ref=buf.at[c], send_sem=send, recv_sem=sems.at[(t + 1) * per + j],
            device_id={"row": to}, device_id_type=MESH)

    def step(t, first=False, last=False):
        c_right = lax.rem(r - t + n_row, n_row) * per
        c_left = lax.rem(r + 1 + t, n_row) * per
        for j in range(per):
            for buf, c, sems, send, to in ((right_buf, c_right + j, right_sem, send_sem.at[0], right),
                                           (left_buf, c_left + j, left_sem, send_sem.at[1], left)):
                if first:
                    buf[c] = own[c]
                else:
                    hop(buf, c, sems, send, t - 1, j, to).wait_recv()
                    buf[c] = buf[c] + own[c]
                if not last:
                    hop(buf, c, sems, send, t, j, to).start()

    step(0, first=True)
    send_x(1)

    def middle(t, carry):
        step(t)
        send_x(2 * t)
        send_x(2 * t + 1)
        return carry

    lax.fori_loop(1, n_row - 1, middle, 0)
    for d in range(2 * n_row - 2, n_wide):
        send_x(d)
    step(n_row - 1, last=True)

    def all_but_one(buf, send, recv, count):
        return pltpu.make_async_remote_copy(
            src_ref=buf.at[pl.ds(0, count)], dst_ref=buf.at[pl.ds(0, count)], send_sem=send, recv_sem=recv,
            device_id={"row": right}, device_id_type=MESH)

    mine.wait()
    x_rows = xs.shape[1] * xs.shape[2]
    other_x = pltpu.make_async_remote_copy(
        src_ref=x_ref.at[pl.ds(0, n_wide - 1)], dst_ref=xs.at[:, pl.ds(0, n_wide - 1)], send_sem=send_sem.at[2],
        recv_sem=x_sem, device_id={"row": right}, device_id_type=MESH)
    other_x.wait_recv()

    acc = None
    for k in range(slabs):
        at = slice(k * STEPS, (k + 1) * STEPS)
        v = (right_buf[at] + left_buf[at] - own[at]).reshape(STEPS * BW, SLAB)
        vs[k] = v
        x = xs[k].reshape(x_rows, SLAB)
        product = dot_t(jnp.concatenate([x, v], axis=0), v)
        acc = product if acc is None else acc + product

    wide = 2 * SLAB
    padded = jnp.concatenate([acc, jnp.zeros((acc.shape[0], wide - acc.shape[1]), jnp.float32)], axis=1)
    first_gram = x_rows // 8
    for peer in range(n_wide):
        i, c = peer // 2, peer % 2
        part[peer, 0] = padded[i * 8:(i + 1) * 8, c * SLAB:(c + 1) * SLAB]
        i, c = GRAM_TILES[peer]
        i = i + first_gram
        part[peer, 1] = padded[i * 8:(i + 1) * 8, c * SLAB:(c + 1) * SLAB]

    def scatter(d, carry):
        peer = lax.rem(w + d, n_wide)
        pltpu.make_async_remote_copy(
            src_ref=part.at[peer], dst_ref=gather_in.at[w], send_sem=send_sem.at[3], recv_sem=red_sem,
            device_id={"wide": peer}, device_id_type=MESH).start()
        return carry

    lax.fori_loop(1, n_wide, scatter, 0)
    gather_in[w] = part[w]
    all_but_one(gather_in, send_sem.at[3], red_sem, n_wide - 1).wait_recv()
    total[...] = jnp.sum(gather_in[...], axis=0)

    def share(d, carry):
        peer = lax.rem(w + d, n_wide)
        pltpu.make_async_remote_copy(
            src_ref=total, dst_ref=gathered.at[w], send_sem=send_sem.at[4], recv_sem=all_sem,
            device_id={"wide": peer}, device_id_type=MESH).start()
        return carry

    lax.fori_loop(1, n_wide, share, 0)
    gathered[w] = total[...]
    all_but_one(gathered, send_sem.at[4], all_sem, n_wide - 1).wait_recv()

    halves = [jnp.concatenate([gathered[2 * i + c, 0] for i in range(n_wide // 2)], axis=0) for c in range(2)]
    inner = jnp.concatenate(halves, axis=1)
    gram0 = jnp.concatenate([gathered[i, 1] for i in range(12)], axis=0)
    gram1 = jnp.concatenate([gathered[i, 1] for i in range(12, 32)], axis=0)
    scaled = []
    for s in range(STEPS):
        at = slice(s * BW, (s + 1) * BW)
        value = inner[:, at]
        gram, first = (gram0, 0) if s < 4 else (gram1, SLAB)
        if s:
            overlap = gram[:s * BW, s * BW - first:(s + 1) * BW - first]
            value = value - dot(jnp.concatenate(scaled, axis=1), overlap)
        scaled.append(dot_t(value, t_ref[s]))
    u = jnp.concatenate(scaled, axis=1)
    for k in range(slabs):
        out_ref[:, k * SLAB:(k + 1) * SLAB] = xs[k].reshape(x_rows, SLAB) - dot(u, vs[k])

    sent = (n_row - 1) * per
    all_but_one(right_buf, send_sem.at[0], right_sem.at[0], sent).wait_send()
    all_but_one(left_buf, send_sem.at[1], left_sem.at[0], sent).wait_send()
    other_x.wait_send()
    all_but_one(part, send_sem.at[3], red_sem, n_wide - 1).wait_send()
    all_but_one(gathered, send_sem.at[4], all_sem, n_wide - 1).wait_send()


def body(n_row, n_wide, eigvec_t, householder, wy_factor, block_place, offsets):
    local = eigvec_t.shape[0]
    ncols = householder.shape[2]
    slabs = ncols // SLAB
    x = eigvec_t.reshape(local, n_wide, slabs, SLAB).transpose(1, 2, 0, 3)
    chunks = slabs * STEPS
    vmem = pl.BlockSpec(memory_space=pltpu.VMEM)
    smem = pl.BlockSpec(memory_space=pltpu.SMEM)
    f32 = jnp.float32
    return pl.pallas_call(
        functools.partial(kernel, n_row, n_wide),
        out_shape=jax.ShapeDtypeStruct((local * n_wide, ncols), f32),
        in_specs=[smem, smem, pl.BlockSpec(memory_space=pl.ANY), vmem, vmem],
        out_specs=vmem,
        scratch_shapes=[
            pltpu.VMEM((chunks, BW, SLAB), f32),
            pltpu.VMEM((chunks, BW, SLAB), f32),
            pltpu.VMEM((chunks, BW, SLAB), f32),
            pltpu.VMEM((slabs, n_wide, local, SLAB), f32),
            pltpu.VMEM((slabs, STEPS * BW, SLAB), f32),
            pltpu.VMEM((n_wide, 2, 8, SLAB), f32),
            pltpu.VMEM((n_wide, 2, 8, SLAB), f32),
            pltpu.VMEM((2, 8, SLAB), f32),
            pltpu.VMEM((n_wide, 2, 8, SLAB), f32),
            pltpu.SemaphoreType.DMA((chunks,)),
            pltpu.SemaphoreType.DMA((chunks,)),
            pltpu.SemaphoreType.DMA,
            pltpu.SemaphoreType.DMA,
            pltpu.SemaphoreType.DMA,
            pltpu.SemaphoreType.DMA((5,)),
            pltpu.SemaphoreType.DMA,
        ],
        compiler_params=pltpu.CompilerParams(collective_id=0, has_side_effects=True, vmem_limit_bytes=32 << 20),
    )(block_place, offsets, x, householder, wy_factor)


def solution(mesh):
    n_row, n_wide = mesh.shape["row"], mesh.shape["wide"]
    return jax.shard_map(
        functools.partial(body, n_row, n_wide),
        mesh=mesh,
        in_specs=(P(("row", "wide"), None), P("row", None, "wide"), P(), P(), P()),
        out_specs=P("row", "wide"),
        check_vma=False,
    )
```

```python
import functools

import jax
import jax.numpy as jnp
from jax import lax
from jax.experimental import pallas as pl
from jax.experimental.pallas import tpu as pltpu
from jax.sharding import PartitionSpec as P

HIGHEST = lax.Precision.HIGHEST
MESH = pl.DeviceIdType.MESH
STEPS, BW, SLAB, CUBE = 6, 32, 128, 4
HALF = STEPS // 2
GRAM_TILES = [(i, 0) for i in range(12)] + [(i, 1) for i in range(20)]


def dot_t(a, b):
    return lax.dot_general(a, b, (((1,), (1,)), ((), ())), precision=HIGHEST, preferred_element_type=jnp.float32)


def dot(a, b):
    return jnp.dot(a, b, precision=HIGHEST, preferred_element_type=jnp.float32)


def kernel(n_row, n_wide, place_ref, offset_ref, x_ref, h_hbm, t_hbm, out_ref,
           h_ref, t_ref, diag, own, feed, flow, vs, xs, part, gather_in, total, gathered,
           feed_sem, flow_sem, done_sem, x_sem, red_sem, all_sem, send_sem, local_sem):
    r = lax.axis_index("row")
    w = lax.axis_index("wide")
    slots = h_ref.shape[0]
    slabs = h_ref.shape[2] // SLAB
    pieces = slabs
    side = pieces * HALF
    q = lax.rem(r, 2)
    a = lax.div(r, 2)
    mine, other = q * side, (1 - q) * side

    def row(delta):
        return lax.rem(r + delta + n_row, n_row)

    near, far = row(1 - 2 * q), row(2 * q - 1)

    barrier = pltpu.get_barrier_semaphore()
    for delta in (1, -1, 2, -2):
        pl.semaphore_signal(barrier, inc=1, device_id={"row": row(delta)}, device_id_type=MESH)

    def greet(d, carry):
        peer = lax.rem(w + d, n_wide)
        pl.semaphore_signal(barrier, inc=1, device_id={"wide": peer}, device_id_type=MESH)
        return carry

    load_h = pltpu.make_async_copy(h_hbm, h_ref, local_sem.at[0])
    load_t = pltpu.make_async_copy(t_hbm, t_ref, local_sem.at[1])
    load_x = pltpu.make_async_copy(x_ref.at[w], xs.at[:, w], local_sem.at[2])
    load_h.start()
    load_t.start()
    load_x.start()
    lax.fori_loop(1, n_wide, greet, 0)
    load_h.wait()

    lane = lax.broadcasted_iota(jnp.int32, (BW, SLAB), 1) + w * (slabs * SLAB)
    for s in range(STEPS):
        place = place_ref[s]
        start = jnp.where(lax.div(place, slots) == r, offset_ref[s], n_wide * slabs * SLAB)
        slot = lax.rem(place, slots)
        for k in range(slabs):
            block = h_ref[slot, :, k * SLAB:(k + 1) * SLAB]
            own[(s // HALF) * side + k * HALF + s % HALF] = jnp.where(lane + k * SLAB >= start, block, 0.0)

    load_t.wait()
    diag[...] = jnp.zeros_like(diag)
    for s in range(STEPS):
        at = s * BW % SLAB
        diag[s * BW // SLAB, at:at + BW, at:at + BW] = t_ref[s]
    pl.semaphore_wait(barrier, n_wide + 3)

    def copy(src, dst, send, recv, to):
        return pltpu.make_async_remote_copy(
            src_ref=src, dst_ref=dst, send_sem=send, recv_sem=recv, device_id=to, device_id_type=MESH)

    def send_feed(i, to):
        for j in range(HALF):
            c = i * HALF + j
            copy(own.at[other + c], feed.at[c], send_sem.at[0], feed_sem.at[c], {"row": to}).start()

    for t in range(pieces // 2):
        i = lax.div(near, 2) - t + pieces
        send_feed(lax.rem(i + lax.rem(i, 2) * (1 + 2 * t), pieces), near)
        i = lax.div(far, 2) - t + pieces
        send_feed(lax.rem(i + (1 - lax.rem(i, 2)) * (1 + 2 * t), pieces), far)

    def send_x(d):
        peer = lax.rem(w + d, n_wide)
        copy(x_ref.at[peer], xs.at[:, w], send_sem.at[2], x_sem, {"wide": peer}).start()

    def hop(t, d, c, j):
        to = row(2 - 4 * d)
        return copy(flow.at[d, c], flow.at[d, c], send_sem.at[1], flow_sem.at[d, (t + 1) * HALF + j], {"row": to})

    def finished(i, c):
        sub = lax.rem(i, 2)
        to = near + sub * (far - near)
        return copy(vs.at[mine + c], vs.at[mine + c], send_sem.at[5], done_sem, {"row": to})

    def advance(t, d, early, first=False, last=False):
        i = lax.rem(a - t + d * (1 + 2 * t) + pieces, pieces)
        for j in range(HALF):
            c = i * HALF + j
            if early:
                copy(own.at[mine + c], feed.at[c], send_sem.at[0], feed_sem.at[c], {"row": near}).wait_recv()
                base = own[mine + c] + feed[c]
                own[mine + c] = base
            else:
                base = own[mine + c]
            if first:
                value = base
            else:
                hop(t - 1, d, c, j).wait_recv()
                value = flow[d, c] + base
            flow[d, c] = value
            if not last:
                hop(t, d, c, j).start()
            if not early:
                vs[mine + c] = value + flow[1 - d, c] - base
                finished(i, c).start()

    def both(t, early, last=False):
        crossed_right = lax.div(r + 2 * n_row, CUBE) - lax.div(r + 2 * n_row - 2 * t, CUBE)
        crossed_left = lax.div(r + 2 * t, CUBE) - lax.div(r, CUBE)
        d = lax.div(crossed_right - crossed_left + 1, 2)
        advance(t, d, early, last=last)
        advance(t, 1 - d, early, last=last)

    def spread(t, carry):
        share = n_wide * 2 // pieces
        lax.fori_loop(t * share, (t + 1) * share, lambda d, c: (send_x(d), c)[1], 0)
        return carry

    advance(0, 0, True, first=True)
    advance(0, 1, True, first=True)
    for d in range(1, n_wide * 2 // pieces):
        send_x(d)

    def early_step(t, carry):
        both(t, True)
        return spread(t, carry)

    def late_step(t, carry):
        both(t, False)
        return carry

    lax.fori_loop(1, pieces // 2, early_step, 0)
    lax.fori_loop(pieces // 2, pieces - 1, late_step, 0)
    both(pieces - 1, False, last=True)

    def total_of(buf, send, recv, count):
        return copy(buf.at[pl.ds(0, count)], buf.at[pl.ds(0, count)], send, recv, {"row": near})

    load_x.wait()
    others = n_wide - 1
    other_x = copy(x_ref.at[pl.ds(0, others)], xs.at[:, pl.ds(0, others)], send_sem.at[2], x_sem, {"row": near})
    other_x.wait_recv()
    x_rows = xs.shape[1] * xs.shape[2]
    all_done = total_of(vs, send_sem.at[5], done_sem, side)
    all_done.wait_recv()

    def slab(k):
        halves = [vs[h * side + k * HALF:h * side + (k + 1) * HALF].reshape(HALF * BW, SLAB) for h in range(2)]
        return jnp.concatenate(halves, axis=0)

    acc = None
    for k in range(slabs):
        v = slab(k)
        x = xs[k].reshape(x_rows, SLAB)
        product = dot_t(jnp.concatenate([x, v], axis=0), v)
        acc = product if acc is None else acc + product

    wide = 2 * SLAB
    padded = jnp.concatenate([acc, jnp.zeros((acc.shape[0], wide - acc.shape[1]), jnp.float32)], axis=1)
    first_gram = x_rows // 8
    for peer in range(n_wide):
        i, c = peer // 2, peer % 2
        part[peer, 0] = padded[i * 8:(i + 1) * 8, c * SLAB:(c + 1) * SLAB]
        i, c = GRAM_TILES[peer]
        i = i + first_gram
        part[peer, 1] = padded[i * 8:(i + 1) * 8, c * SLAB:(c + 1) * SLAB]

    def scatter(d, carry):
        peer = lax.rem(w + d, n_wide)
        copy(part.at[peer], gather_in.at[w], send_sem.at[3], red_sem, {"wide": peer}).start()
        return carry

    lax.fori_loop(1, n_wide, scatter, 0)
    gather_in[w] = part[w]
    parts_in = total_of(gather_in, send_sem.at[3], red_sem, others)
    parts_in.wait_recv()
    total[...] = jnp.sum(gather_in[...], axis=0)

    def share(d, carry):
        peer = lax.rem(w + d, n_wide)
        copy(total, gathered.at[w], send_sem.at[4], all_sem, {"wide": peer}).start()
        return carry

    lax.fori_loop(1, n_wide, share, 0)
    gathered[w] = total[...]
    totals_in = total_of(gathered, send_sem.at[4], all_sem, others)
    totals_in.wait_recv()

    solved = []
    for c in range(2):
        rows = [gathered[2 * i + c, 0] for i in range(n_wide // 2)]
        rows += [gathered[i, 1] for i in range(n_wide) if GRAM_TILES[i][1] == c]
        solved.append(dot_t(jnp.concatenate(rows, axis=0), diag[c]))
    scaled = []
    for s in range(STEPS):
        c, at = s * BW // SLAB, s * BW % SLAB
        value = solved[c][:x_rows, at:at + BW]
        if s:
            value = value - dot(jnp.concatenate(scaled, axis=1), solved[c][x_rows:x_rows + s * BW, at:at + BW])
        scaled.append(value)
    u = jnp.concatenate(scaled, axis=1)
    for k in range(0, slabs, 2):
        v = jnp.concatenate([slab(k), slab(k + 1)], axis=1)
        x = jnp.concatenate([xs[k].reshape(x_rows, SLAB), xs[k + 1].reshape(x_rows, SLAB)], axis=1)
        out_ref[:, k * SLAB:(k + 2) * SLAB] = x - dot(u, v)

    total_of(own, send_sem.at[0], feed_sem.at[0], side).wait_send()
    copy(flow.at[:, pl.ds(0, side - HALF)], flow.at[:, pl.ds(0, side - HALF)], send_sem.at[1], feed_sem.at[0],
         {"row": near}).wait_send()
    other_x.wait_send()
    all_done.wait_send()
    parts_in.wait_send()
    totals_in.wait_send()


def body(n_row, n_wide, eigvec_t, householder, wy_factor, block_place, offsets):
    local = eigvec_t.shape[0]
    ncols = householder.shape[2]
    slabs = ncols // SLAB
    side = slabs * HALF
    x = eigvec_t.reshape(local, n_wide, slabs, SLAB).transpose(1, 2, 0, 3)
    smem = pl.BlockSpec(memory_space=pltpu.SMEM)
    hbm = pl.BlockSpec(memory_space=pl.ANY)
    f32 = jnp.float32
    return pl.pallas_call(
        functools.partial(kernel, n_row, n_wide),
        out_shape=jax.ShapeDtypeStruct((local * n_wide, ncols), f32),
        in_specs=[smem, smem, hbm, hbm, hbm],
        out_specs=pl.BlockSpec(memory_space=pltpu.VMEM),
        scratch_shapes=[
            pltpu.VMEM(householder.shape, f32),
            pltpu.VMEM(wy_factor.shape, f32),
            pltpu.VMEM((2, SLAB, SLAB), f32),
            pltpu.VMEM((2 * side, BW, SLAB), f32),
            pltpu.VMEM((side, BW, SLAB), f32),
            pltpu.VMEM((2, side, BW, SLAB), f32),
            pltpu.VMEM((2 * side, BW, SLAB), f32),
            pltpu.VMEM((slabs, n_wide, local, SLAB), f32),
            pltpu.VMEM((n_wide, 2, 8, SLAB), f32),
            pltpu.VMEM((n_wide, 2, 8, SLAB), f32),
            pltpu.VMEM((2, 8, SLAB), f32),
            pltpu.VMEM((n_wide, 2, 8, SLAB), f32),
            pltpu.SemaphoreType.DMA((side,)),
            pltpu.SemaphoreType.DMA((2, side)),
            pltpu.SemaphoreType.DMA,
            pltpu.SemaphoreType.DMA,
            pltpu.SemaphoreType.DMA,
            pltpu.SemaphoreType.DMA,
            pltpu.SemaphoreType.DMA((6,)),
            pltpu.SemaphoreType.DMA((3,)),
        ],
        compiler_params=pltpu.CompilerParams(collective_id=0, has_side_effects=True, vmem_limit_bytes=60 << 20),
    )(block_place, offsets, x, householder, wy_factor)


def solution(mesh):
    n_row, n_wide = mesh.shape["row"], mesh.shape["wide"]
    return jax.shard_map(
        functools.partial(body, n_row, n_wide),
        mesh=mesh,
        in_specs=(P(("row", "wide"), None), P("row", None, "wide"), P(), P(), P()),
        out_specs=P("row", "wide"),
        check_vma=False,
    )
```

```python
import functools

import jax
import jax.numpy as jnp
from jax import lax
from jax.experimental import pallas as pl
from jax.experimental.pallas import tpu as pltpu
from jax.sharding import PartitionSpec as P

HIGHEST = lax.Precision.HIGHEST
MESH = pl.DeviceIdType.MESH
STEPS, BW, SLAB, CUBE = 6, 32, 128, 4
HALF = STEPS // 2
GRAM_TILES = [(i, 0) for i in range(12)] + [(i, 1) for i in range(20)]


def dot_t(a, b):
    return lax.dot_general(a, b, (((1,), (1,)), ((), ())), precision=HIGHEST, preferred_element_type=jnp.float32)


def dot(a, b):
    return jnp.dot(a, b, precision=HIGHEST, preferred_element_type=jnp.float32)


def kernel(n_row, n_wide, place_hbm, offset_hbm, x_ref, h_hbm, t_hbm, out_ref,
           place_ref, offset_ref, h_ref, t_ref, diag, own, feed, flow, vs, xs,
           part, core_in, pair, gather_in, total, gathered,
           feed_sem, flow_sem, done_sem, x_sem, core_sem, red_sem, all_sem, send_sem, local_sem):
    r = lax.axis_index("row")
    w = lax.axis_index("wide")
    slots = h_ref.shape[0]
    slabs = h_ref.shape[2] // SLAB
    pieces = slabs
    side = pieces * HALF
    q = lax.rem(r, 2)
    a = lax.div(r, 2)
    mine, other = q * side, (1 - q) * side

    def row(delta):
        return lax.rem(r + delta + n_row, n_row)

    near, far = row(1 - 2 * q), row(2 * q - 1)

    barrier = pltpu.get_barrier_semaphore()
    for delta in (1, -1, 2, -2):
        pl.semaphore_signal(barrier, inc=1, device_id={"row": row(delta)}, device_id_type=MESH)

    def greet(d, carry):
        peer = lax.rem(w + d, n_wide)
        pl.semaphore_signal(barrier, inc=1, device_id={"wide": peer}, device_id_type=MESH)
        return carry

    load_h = pltpu.make_async_copy(h_hbm, h_ref, local_sem.at[0])
    load_t = pltpu.make_async_copy(t_hbm, t_ref, local_sem.at[1])
    load_x = pltpu.make_async_copy(x_ref.at[w], xs.at[:, w], local_sem.at[2])
    load_place = pltpu.make_async_copy(place_hbm, place_ref, local_sem.at[3])
    load_offset = pltpu.make_async_copy(offset_hbm, offset_ref, local_sem.at[4])
    load_place.start()
    load_offset.start()
    load_h.start()
    load_t.start()
    load_x.start()
    lax.fori_loop(1, n_wide, greet, 0)
    load_place.wait()
    load_offset.wait()
    load_h.wait()

    lane = lax.broadcasted_iota(jnp.int32, (BW, SLAB), 1) + w * (slabs * SLAB)
    for s in range(STEPS):
        place = place_ref[s]
        start = jnp.where(lax.div(place, slots) == r, offset_ref[s], n_wide * slabs * SLAB)
        slot = lax.rem(place, slots)
        for k in range(slabs):
            block = h_ref[slot, :, k * SLAB:(k + 1) * SLAB]
            own[k * STEPS + s] = jnp.where(lane + k * SLAB >= start, block, 0.0)

    load_t.wait()
    diag[...] = jnp.zeros_like(diag)
    for s in range(STEPS):
        at = s * BW % SLAB
        diag[s * BW // SLAB, at:at + BW, at:at + BW] = t_ref[s]
    pl.semaphore_wait(barrier, n_wide + 3)

    def copy(src, dst, send, recv, to):
        return pltpu.make_async_remote_copy(
            src_ref=src, dst_ref=dst, send_sem=send, recv_sem=recv, device_id=to, device_id_type=MESH)

    def send_feed(i, to):
        for j in range(HALF):
            c = i * HALF + j
            copy(own.at[other + c], feed.at[c], send_sem.at[0], feed_sem.at[c], {"row": to}).start()

    for t in range(pieces // 2):
        i = lax.div(near, 2) - t + pieces
        send_feed(lax.rem(i + lax.rem(i, 2) * (1 + 2 * t), pieces), near)
        i = lax.div(far, 2) - t + pieces
        send_feed(lax.rem(i + (1 - lax.rem(i, 2)) * (1 + 2 * t), pieces), far)

    def send_x(d):
        peer = lax.rem(w + d, n_wide)
        copy(x_ref.at[peer], xs.at[:, w], send_sem.at[2], x_sem, {"wide": peer}).start()

    def hop(t, d, c, j):
        to = row(2 - 4 * d)
        return copy(flow.at[d, c], flow.at[d, c], send_sem.at[1], flow_sem.at[d, (t + 1) * HALF + j], {"row": to})

    def finished(i, c):
        sub = lax.rem(i, 2)
        to = near + sub * (far - near)
        return copy(vs.at[mine + c], vs.at[mine + c], send_sem.at[5], done_sem, {"row": to})

    def advance(t, d, early, first=False, last=False):
        i = lax.rem(a - t + d * (1 + 2 * t) + pieces, pieces)
        for j in range(HALF):
            c = i * HALF + j
            if early:
                copy(own.at[mine + c], feed.at[c], send_sem.at[0], feed_sem.at[c], {"row": near}).wait_recv()
                base = own[mine + c] + feed[c]
                own[mine + c] = base
            else:
                base = own[mine + c]
            if first:
                value = base
            else:
                hop(t - 1, d, c, j).wait_recv()
                value = flow[d, c] + base
            flow[d, c] = value
            if not last:
                hop(t, d, c, j).start()
            if not early:
                vs[mine + c] = value + flow[1 - d, c] - base
                finished(i, c).start()

    def both(t, early, last=False):
        crossed_right = lax.div(r + 2 * n_row, CUBE) - lax.div(r + 2 * n_row - 2 * t, CUBE)
        crossed_left = lax.div(r + 2 * t, CUBE) - lax.div(r, CUBE)
        d = lax.div(crossed_right - crossed_left + 1, 2)
        advance(t, d, early, last=last)
        advance(t, 1 - d, early, last=last)

    def spread(t, carry):
        share = n_wide * 2 // pieces
        lax.fori_loop(t * share, (t + 1) * share, lambda d, c: (send_x(d), c)[1], 0)
        return carry

    advance(0, 0, True, first=True)
    advance(0, 1, True, first=True)
    for d in range(1, n_wide * 2 // pieces):
        send_x(d)

    def early_step(t, carry):
        both(t, True)
        return spread(t, carry)

    def late_step(t, carry):
        both(t, False)
        return carry

    lax.fori_loop(1, pieces // 2, early_step, 0)
    lax.fori_loop(pieces // 2, pieces - 1, late_step, 0)
    both(pieces - 1, False, last=True)

    def total_of(buf, send, recv, count):
        return copy(buf.at[pl.ds(0, count)], buf.at[pl.ds(0, count)], send, recv, {"row": near})

    load_x.wait()
    others = n_wide - 1
    other_x = copy(x_ref.at[pl.ds(0, others)], xs.at[:, pl.ds(0, others)], send_sem.at[2], x_sem, {"row": near})
    other_x.wait_recv()
    x_rows = xs.shape[1] * xs.shape[2]
    all_done = total_of(vs, send_sem.at[5], done_sem, side)

    def slab(k):
        return vs[pl.ds(k * STEPS, STEPS)].reshape(STEPS * BW, SLAB)

    def products(first):
        acc = None
        for m in range(slabs // 2):
            v = slab(first + m)
            x = xs[first + m].reshape(x_rows, SLAB)
            product = dot_t(jnp.concatenate([x, v], axis=0), v)
            acc = product if acc is None else acc + product
        return acc

    acc = products(q * (slabs // 2))
    all_done.wait_recv()
    acc = acc + products((1 - q) * (slabs // 2))

    wide = 2 * SLAB
    padded = jnp.concatenate([acc, jnp.zeros((acc.shape[0], wide - acc.shape[1]), jnp.float32)], axis=1)
    first_gram = x_rows // 8
    core = lax.rem(w, 2)
    chip = lax.div(w, 2)
    twin = w + 1 - 2 * core
    chips = n_wide // 2
    for i in range(chips):
        for c in range(2):
            part[c, i, 0] = padded[i * 8:(i + 1) * 8, c * SLAB:(c + 1) * SLAB]
            tile, column = GRAM_TILES[2 * i + c]
            tile = tile + first_gram
            part[c, i, 1] = padded[tile * 8:(tile + 1) * 8, column * SLAB:(column + 1) * SLAB]

    to_twin = copy(part.at[1 - core], core_in, send_sem.at[6], core_sem.at[0], {"wide": twin})
    to_twin.start()
    to_twin.wait_recv()
    pair[...] = part[core] + core_in[...]

    around = sorted(((dx, dy) for dx in range(4) for dy in range(4) if dx or dy),
                    key=lambda at: -min(at[0], 4 - at[0]) - min(at[1], 4 - at[1]))

    def chip_at(dx, dy):
        return lax.rem(lax.div(chip, 4) + dx, 4) * 4 + lax.rem(lax.rem(chip, 4) + dy, 4)

    for dx, dy in around:
        to = chip_at(dx, dy)
        copy(pair.at[to], gather_in.at[chip], send_sem.at[3], red_sem, {"wide": 2 * to + core}).start()
    gather_in[chip] = pair[chip]
    parts_in = total_of(gather_in, send_sem.at[3], red_sem, chips - 1)
    parts_in.wait_recv()
    total[...] = jnp.sum(gather_in[...], axis=0)

    for dx, dy in around:
        to = chip_at(dx, dy)
        copy(total, gathered.at[core, chip], send_sem.at[4], all_sem, {"wide": 2 * to + core}).start()
    gathered[core, chip] = total[...]
    totals_in = total_of(gather_in, send_sem.at[4], all_sem, chips - 1)
    totals_in.wait_recv()
    all_to_twin = copy(gathered.at[core], gathered.at[core], send_sem.at[7], core_sem.at[1], {"wide": twin})
    all_to_twin.start()
    all_to_twin.wait_recv()

    solved = []
    for c in range(2):
        rows = [gathered[c, i, 0] for i in range(chips)]
        rows += [gathered[i % 2, i // 2, 1] for i in range(n_wide) if GRAM_TILES[i][1] == c]
        solved.append(dot_t(jnp.concatenate(rows, axis=0), diag[c]))
    scaled = []
    for s in range(STEPS):
        c, at = s * BW // SLAB, s * BW % SLAB
        value = solved[c][:x_rows, at:at + BW]
        if s:
            value = value - dot(jnp.concatenate(scaled, axis=1), solved[c][x_rows:x_rows + s * BW, at:at + BW])
        scaled.append(value)
    u = jnp.concatenate(scaled, axis=1)
    for k in range(0, slabs, 2):
        v = jnp.concatenate([slab(k), slab(k + 1)], axis=1)
        x = jnp.concatenate([xs[k].reshape(x_rows, SLAB), xs[k + 1].reshape(x_rows, SLAB)], axis=1)
        out_ref[:, k * SLAB:(k + 2) * SLAB] = x - dot(u, v)

    total_of(own, send_sem.at[0], feed_sem.at[0], side).wait_send()
    copy(flow.at[:, pl.ds(0, side - HALF)], flow.at[:, pl.ds(0, side - HALF)], send_sem.at[1], feed_sem.at[0],
         {"row": near}).wait_send()
    other_x.wait_send()
    all_done.wait_send()
    parts_in.wait_send()
    totals_in.wait_send()
    to_twin.wait_send()
    all_to_twin.wait_send()


def body(n_row, n_wide, eigvec_t, householder, wy_factor, block_place, offsets):
    local = eigvec_t.shape[0]
    ncols = householder.shape[2]
    slabs = ncols // SLAB
    side = slabs * HALF
    x = eigvec_t.reshape(local, n_wide, slabs, SLAB).transpose(1, 2, 0, 3)
    chips = n_wide // 2
    hbm = pl.BlockSpec(memory_space=pltpu.HBM)
    operands = [pltpu.with_memory_space_constraint(v, pltpu.HBM)
                for v in (block_place, offsets, x, householder, wy_factor)]
    f32 = jnp.float32
    return pl.pallas_call(
        functools.partial(kernel, n_row, n_wide),
        out_shape=jax.ShapeDtypeStruct((local * n_wide, ncols), f32),
        in_specs=[hbm] * 5,
        out_specs=pl.BlockSpec(memory_space=pltpu.VMEM),
        scratch_shapes=[
            pltpu.SMEM(block_place.shape, jnp.int32),
            pltpu.SMEM(offsets.shape, jnp.int32),
            pltpu.VMEM(householder.shape, f32),
            pltpu.VMEM(wy_factor.shape, f32),
            pltpu.VMEM((2, SLAB, SLAB), f32),
            pltpu.VMEM((2 * side, BW, SLAB), f32),
            pltpu.VMEM((side, BW, SLAB), f32),
            pltpu.VMEM((2, side, BW, SLAB), f32),
            pltpu.VMEM((2 * side, BW, SLAB), f32),
            pltpu.VMEM((slabs, n_wide, local, SLAB), f32),
            pltpu.VMEM((2, chips, 2, 8, SLAB), f32),
            pltpu.VMEM((chips, 2, 8, SLAB), f32),
            pltpu.VMEM((chips, 2, 8, SLAB), f32),
            pltpu.VMEM((chips, 2, 8, SLAB), f32),
            pltpu.VMEM((2, 8, SLAB), f32),
            pltpu.VMEM((2, chips, 2, 8, SLAB), f32),
            pltpu.SemaphoreType.DMA((side,)),
            pltpu.SemaphoreType.DMA((2, side)),
            pltpu.SemaphoreType.DMA,
            pltpu.SemaphoreType.DMA,
            pltpu.SemaphoreType.DMA((2,)),
            pltpu.SemaphoreType.DMA,
            pltpu.SemaphoreType.DMA,
            pltpu.SemaphoreType.DMA((8,)),
            pltpu.SemaphoreType.DMA((5,)),
        ],
        compiler_params=pltpu.CompilerParams(collective_id=0, has_side_effects=True, vmem_limit_bytes=32 << 20),
    )(*operands)


def solution(mesh):
    n_row, n_wide = mesh.shape["row"], mesh.shape["wide"]
    return jax.shard_map(
        functools.partial(body, n_row, n_wide),
        mesh=mesh,
        in_specs=(P(("row", "wide"), None), P("row", None, "wide"), P(), P(), P()),
        out_specs=P("row", "wide"),
        check_vma=False,
    )
```

```python
import functools

import jax
import jax.numpy as jnp
from jax import lax
from jax.experimental import pallas as pl
from jax.experimental.pallas import tpu as pltpu
from jax.sharding import PartitionSpec as P

HIGHEST = lax.Precision.HIGHEST
MESH = pl.DeviceIdType.MESH
STEPS, BW, SLAB, CUBE = 6, 32, 128, 4
PIECE = STEPS // 2 * BW
CUTS = 3
CHUNK = PIECE // CUTS
GRAM_TILES = [(i, 0) for i in range(12)] + [(i, 1) for i in range(20)]


def dot_t(a, b):
    return lax.dot_general(a, b, (((1,), (1,)), ((), ())), precision=HIGHEST, preferred_element_type=jnp.float32)


def dot(a, b):
    return jnp.dot(a, b, precision=HIGHEST, preferred_element_type=jnp.float32)


def kernel(n_row, n_wide, place_hbm, offset_hbm, x_ref, h_hbm, t_hbm, out_ref,
           place_ref, offset_ref, h_ref, t_ref, diag, own, feed, flow, vs, xs,
           part, core_in, pair, gather_in, total, gathered,
           feed_sem, flow_sem, done_sem, x_sem, core_sem, red_sem, all_sem, send_sem, local_sem):
    r = lax.axis_index("row")
    w = lax.axis_index("wide")
    slots = h_ref.shape[0]
    slabs = h_ref.shape[2] // SLAB
    pieces = slabs
    side = pieces * PIECE
    q = lax.rem(r, 2)
    a = lax.div(r, 2)
    mine, other = q * side, (1 - q) * side

    def row(delta):
        return lax.rem(r + delta + n_row, n_row)

    near, far = row(1 - 2 * q), row(2 * q - 1)

    barrier = pltpu.get_barrier_semaphore()
    for delta in (1, -1, 2, -2):
        pl.semaphore_signal(barrier, inc=1, device_id={"row": row(delta)}, device_id_type=MESH)

    def greet(d, carry):
        peer = lax.rem(w + d, n_wide)
        pl.semaphore_signal(barrier, inc=1, device_id={"wide": peer}, device_id_type=MESH)
        return carry

    load_h = pltpu.make_async_copy(h_hbm, h_ref, local_sem.at[0])
    load_t = pltpu.make_async_copy(t_hbm, t_ref, local_sem.at[1])
    load_x = pltpu.make_async_copy(x_ref.at[w], xs.at[:, w], local_sem.at[2])
    load_place = pltpu.make_async_copy(place_hbm, place_ref, local_sem.at[3])
    load_offset = pltpu.make_async_copy(offset_hbm, offset_ref, local_sem.at[4])
    load_place.start()
    load_offset.start()
    load_h.start()
    load_t.start()
    load_x.start()
    lax.fori_loop(1, n_wide, greet, 0)
    load_place.wait()
    load_offset.wait()
    load_h.wait()

    lane = lax.broadcasted_iota(jnp.int32, (BW, SLAB), 1) + w * (slabs * SLAB)
    for s in range(STEPS):
        place = place_ref[s]
        start = jnp.where(lax.div(place, slots) == r, offset_ref[s], n_wide * slabs * SLAB)
        slot = lax.rem(place, slots)
        for k in range(slabs):
            block = h_ref[slot, :, k * SLAB:(k + 1) * SLAB]
            own[pl.ds((k * STEPS + s) * BW, BW)] = jnp.where(lane + k * SLAB >= start, block, 0.0)

    pl.semaphore_wait(barrier, n_wide + 3)

    def copy(src, dst, send, recv, to):
        return pltpu.make_async_remote_copy(
            src_ref=src, dst_ref=dst, send_sem=send, recv_sem=recv, device_id=to, device_id_type=MESH)

    def span(start, size):
        return pl.ds(pl.multiple_of(start, 8), size)

    def send_feed(t):
        for to, odd in ((near, 0), (far, 1)):
            i = lax.div(to, 2) - t + pieces
            i = lax.rem(i + lax.rem(i + odd, 2) * (1 + 2 * t), pieces)
            for at, size, n in chunks_of(i, isinstance(t, int)):
                copy(own.at[span(other + at, size)], feed.at[span(at, size)], send_sem.at[0], feed_sem.at[n],
                     {"row": to}).start()

    def chunks_of(i, single):
        return [(i * PIECE + j * CHUNK, CHUNK, i * CUTS + j) for j in range(CUTS)] if single else [(i * PIECE, PIECE, i * CUTS)]

    def send_x(d):
        peer = lax.rem(w + d, n_wide)
        copy(x_ref.at[peer], xs.at[:, w], send_sem.at[2], x_sem, {"wide": peer}).start()

    def hop(t, d, at, j):
        buf = flow.at[d, span(at, CHUNK)]
        return copy(buf, buf, send_sem.at[1], flow_sem.at[d, (t + 1) * CUTS + j], {"row": row(2 - 4 * d)})

    def send_finished(t, d, single):
        i = piece(t, d)
        to = near + lax.rem(i, 2) * (far - near)
        for at, size, n in chunks_of(i, single):
            here, flowed = span(mine + at, size), span(at, size)
            vs[here] = flow[0, flowed] + flow[1, flowed] - own[here]
            copy(vs.at[here], vs.at[here], send_sem.at[5], done_sem, {"row": to}).start()

    def piece(t, d):
        return lax.rem(a - t + d * (1 + 2 * t) + pieces, pieces)

    def add_feed(t, d, single):
        for at, size, n in chunks_of(piece(t, d), single):
            here, fed = span(mine + at, size), span(at, size)
            copy(own.at[here], feed.at[fed], send_sem.at[0], feed_sem.at[n], {"row": near}).wait_recv()
            own[here] = own[here] + feed[fed]

    def advance(t, d, first=False, last=False):
        for j in range(CUTS):
            at = piece(t, d) * PIECE + j * CHUNK
            here, flowed = span(mine + at, CHUNK), span(at, CHUNK)
            if first:
                flow[d, flowed] = own[here]
            else:
                hop(t - 1, d, at, j).wait_recv()
                flow[d, flowed] = flow[d, flowed] + own[here]
            if not last:
                hop(t, d, at, j).start()

    def first_stream(t):
        crossed_right = lax.div(r + 2 * n_row, CUBE) - lax.div(r + 2 * n_row - 2 * t, CUBE)
        crossed_left = lax.div(r + 2 * t, CUBE) - lax.div(r, CUBE)
        return lax.div(crossed_right - crossed_left + 1, 2)

    def spread(t):
        share = n_wide * 2 // pieces
        lax.fori_loop(t * share, (t + 1) * share, lambda d, c: (send_x(d), c)[1], 0)

    def early_step(t, carry):
        for d in range(2):
            add_feed(t, d, False)
        d = first_stream(t)
        advance(t, d)
        advance(t, 1 - d)
        pl.when(t < pieces // 2 - 2)(lambda: send_feed(t + 2))
        spread(t)
        return carry

    def late_step(t, carry):
        d = first_stream(t)
        advance(t, d)
        advance(t, 1 - d)
        send_finished(t, d, True)
        send_finished(t, 1 - d, True)
        return carry

    send_feed(0)
    send_feed(jnp.int32(1))
    for d in range(2):
        add_feed(0, d, True)
        advance(0, d, first=True)
    send_feed(jnp.int32(2))
    for d in range(1, n_wide * 2 // pieces):
        send_x(d)
    lax.fori_loop(1, pieces // 2, early_step, 0)
    lax.fori_loop(pieces // 2, pieces - 1, late_step, 0)
    d = first_stream(pieces - 1)
    for d in (d, 1 - d):
        advance(pieces - 1, d, last=True)
        send_finished(pieces - 1, d, True)

    def total_of(buf, send, recv, count):
        return copy(buf.at[pl.ds(0, count)], buf.at[pl.ds(0, count)], send, recv, {"row": near})

    load_t.wait()
    diag[...] = jnp.zeros_like(diag)
    for s in range(STEPS):
        at = s * BW % SLAB
        diag[s * BW // SLAB, at:at + BW, at:at + BW] = t_ref[s]
    load_x.wait()
    others = n_wide - 1
    other_x = copy(x_ref.at[pl.ds(0, others)], xs.at[:, pl.ds(0, others)], send_sem.at[2], x_sem, {"row": near})
    other_x.wait_recv()
    x_rows = xs.shape[1] * xs.shape[2]
    all_done = total_of(vs, send_sem.at[5], done_sem, side)

    def slab(k):
        return vs[span(k * (STEPS * BW), STEPS * BW)]

    def x_slab(k):
        return xs[k].reshape(x_rows, SLAB)

    def pair_of(part_of, k):
        return jnp.concatenate([part_of(k), part_of(k + 1)], axis=1)

    def products(first):
        acc = None
        for m in range(0, slabs // 2, 2):
            v, x = pair_of(slab, first + m), pair_of(x_slab, first + m)
            product = dot_t(jnp.concatenate([x, v], axis=0), v)
            acc = product if acc is None else acc + product
        return acc

    acc = products(q * (slabs // 2))
    all_done.wait_recv()
    acc = acc + products((1 - q) * (slabs // 2))

    wide = 2 * SLAB
    padded = jnp.concatenate([acc, jnp.zeros((acc.shape[0], wide - acc.shape[1]), jnp.float32)], axis=1)
    first_gram = x_rows // 8
    core = lax.rem(w, 2)
    chip = lax.div(w, 2)
    twin = w + 1 - 2 * core
    chips = n_wide // 2
    for i in range(chips):
        for c in range(2):
            part[c, i, 0] = padded[i * 8:(i + 1) * 8, c * SLAB:(c + 1) * SLAB]
            tile, column = GRAM_TILES[2 * i + c]
            tile = tile + first_gram
            part[c, i, 1] = padded[tile * 8:(tile + 1) * 8, column * SLAB:(column + 1) * SLAB]

    to_twin = copy(part.at[1 - core], core_in, send_sem.at[6], core_sem.at[0], {"wide": twin})
    to_twin.start()
    to_twin.wait_recv()
    pair[...] = part[core] + core_in[...]

    around = sorted(((dx, dy) for dx in range(4) for dy in range(4) if dx or dy),
                    key=lambda at: -min(at[0], 4 - at[0]) - min(at[1], 4 - at[1]))

    def chip_at(dx, dy):
        return lax.rem(lax.div(chip, 4) + dx, 4) * 4 + lax.rem(lax.rem(chip, 4) + dy, 4)

    for dx, dy in around:
        to = chip_at(dx, dy)
        copy(pair.at[to], gather_in.at[chip], send_sem.at[3], red_sem, {"wide": 2 * to + core}).start()
    gather_in[chip] = pair[chip]
    parts_in = total_of(gather_in, send_sem.at[3], red_sem, chips - 1)
    parts_in.wait_recv()
    total[...] = jnp.sum(gather_in[...], axis=0)

    for dx, dy in around:
        to = chip_at(dx, dy)
        copy(total, gathered.at[core, chip], send_sem.at[4], all_sem, {"wide": 2 * to + core}).start()
    gathered[core, chip] = total[...]
    totals_in = total_of(gather_in, send_sem.at[4], all_sem, chips - 1)
    totals_in.wait_recv()
    all_to_twin = copy(gathered.at[core], gathered.at[core], send_sem.at[7], core_sem.at[1], {"wide": twin})
    all_to_twin.start()
    all_to_twin.wait_recv()

    solved = []
    for c in range(2):
        rows = [gathered[c, i, 0] for i in range(chips)]
        rows += [gathered[i % 2, i // 2, 1] for i in range(n_wide) if GRAM_TILES[i][1] == c]
        solved.append(dot_t(jnp.concatenate(rows, axis=0), diag[c]))
    scaled = []
    for s in range(STEPS):
        c, at = s * BW // SLAB, s * BW % SLAB
        value = solved[c][:x_rows, at:at + BW]
        if s:
            value = value - dot(jnp.concatenate(scaled, axis=1), solved[c][x_rows:x_rows + s * BW, at:at + BW])
        scaled.append(value)
    u = jnp.concatenate(scaled, axis=1)
    for k in range(0, slabs, 2):
        out_ref[:, k * SLAB:(k + 2) * SLAB] = pair_of(x_slab, k) - dot(u, pair_of(slab, k))

    total_of(own, send_sem.at[0], feed_sem.at[0], side).wait_send()
    copy(flow.at[:, pl.ds(0, side - PIECE)], flow.at[:, pl.ds(0, side - PIECE)], send_sem.at[1], feed_sem.at[0],
         {"row": near}).wait_send()
    other_x.wait_send()
    all_done.wait_send()
    parts_in.wait_send()
    totals_in.wait_send()
    to_twin.wait_send()
    all_to_twin.wait_send()


def body(n_row, n_wide, eigvec_t, householder, wy_factor, block_place, offsets):
    local = eigvec_t.shape[0]
    ncols = householder.shape[2]
    slabs = ncols // SLAB
    side = slabs * PIECE
    x = eigvec_t.reshape(local, n_wide, slabs, SLAB).transpose(1, 2, 0, 3)
    chips = n_wide // 2
    hbm = pl.BlockSpec(memory_space=pltpu.HBM)
    operands = [pltpu.with_memory_space_constraint(v, pltpu.HBM)
                for v in (block_place, offsets, x, householder, wy_factor)]
    f32 = jnp.float32
    return pl.pallas_call(
        functools.partial(kernel, n_row, n_wide),
        out_shape=jax.ShapeDtypeStruct((local * n_wide, ncols), f32),
        in_specs=[hbm] * 5,
        out_specs=pl.BlockSpec(memory_space=pltpu.VMEM),
        scratch_shapes=[
            pltpu.SMEM(block_place.shape, jnp.int32),
            pltpu.SMEM(offsets.shape, jnp.int32),
            pltpu.VMEM(householder.shape, f32),
            pltpu.VMEM(wy_factor.shape, f32),
            pltpu.VMEM((2, SLAB, SLAB), f32),
            pltpu.VMEM((2 * side, SLAB), f32),
            pltpu.VMEM((side, SLAB), f32),
            pltpu.VMEM((2, side, SLAB), f32),
            pltpu.VMEM((2 * side, SLAB), f32),
            pltpu.VMEM((slabs, n_wide, local, SLAB), f32),
            pltpu.VMEM((2, chips, 2, 8, SLAB), f32),
            pltpu.VMEM((chips, 2, 8, SLAB), f32),
            pltpu.VMEM((chips, 2, 8, SLAB), f32),
            pltpu.VMEM((chips, 2, 8, SLAB), f32),
            pltpu.VMEM((2, 8, SLAB), f32),
            pltpu.VMEM((2, chips, 2, 8, SLAB), f32),
            pltpu.SemaphoreType.DMA((slabs * CUTS,)),
            pltpu.SemaphoreType.DMA((2, slabs * CUTS)),
            pltpu.SemaphoreType.DMA,
            pltpu.SemaphoreType.DMA,
            pltpu.SemaphoreType.DMA((2,)),
            pltpu.SemaphoreType.DMA,
            pltpu.SemaphoreType.DMA,
            pltpu.SemaphoreType.DMA((8,)),
            pltpu.SemaphoreType.DMA((5,)),
        ],
        compiler_params=pltpu.CompilerParams(collective_id=0, has_side_effects=True, vmem_limit_bytes=32 << 20),
    )(*operands)


def solution(mesh):
    n_row, n_wide = mesh.shape["row"], mesh.shape["wide"]
    return jax.shard_map(
        functools.partial(body, n_row, n_wide),
        mesh=mesh,
        in_specs=(P(("row", "wide"), None), P("row", None, "wide"), P(), P(), P()),
        out_specs=P("row", "wide"),
        check_vma=False,
    )
```

```python
import functools

import jax
import jax.numpy as jnp
from jax import lax
from jax.experimental import pallas as pl
from jax.experimental.pallas import tpu as pltpu
from jax.sharding import PartitionSpec as P

HIGHEST = lax.Precision.HIGHEST
MESH = pl.DeviceIdType.MESH
STEPS, BW, SLAB, CUBE = 6, 32, 128, 4
FREE = STEPS - 2
CUTS = FREE // 2
LINES, LAG = 1, 1
PIECE = CUTS * BW
CHUNK = BW
GRAM_TILES = [(i, 0) for i in range(12)] + [(i, 1) for i in range(20)]


def dot_t(a, b):
    return lax.dot_general(a, b, (((1,), (1,)), ((), ())), precision=HIGHEST, preferred_element_type=jnp.float32)


def dot(a, b):
    return jnp.dot(a, b, precision=HIGHEST, preferred_element_type=jnp.float32)


def kernel(n_row, n_wide, place_hbm, offset_hbm, x_ref, h_hbm, t_hbm, out_ref,
           place_ref, offset_ref, h_ref, t_ref, diag, own, feed, flow, mine_v, other_v, xs,
           part, core_in, pair, gather_in, total, gathered,
           feed_sem, flow_sem, done_sem, fixed_sem, fixed_done_sem, x_sem, core_sem, red_sem, all_sem, send_sem, local_sem):
    r = lax.axis_index("row")
    w = lax.axis_index("wide")
    slots = h_ref.shape[0]
    slabs = h_ref.shape[2] // SLAB
    pieces = slabs
    side = pieces * PIECE
    q = lax.rem(r, 2)
    a = lax.div(r, 2)
    mine, other = q * side, (1 - q) * side

    def row(delta):
        return lax.rem(r + delta + n_row, n_row)

    near, far = row(1 - 2 * q), row(2 * q - 1)

    barrier = pltpu.get_barrier_semaphore()
    for delta in (1, -1, 2, -2):
        pl.semaphore_signal(barrier, inc=1, device_id={"row": row(delta)}, device_id_type=MESH)

    def greet(d, carry):
        peer = lax.rem(w + d, n_wide)
        pl.semaphore_signal(barrier, inc=1, device_id={"wide": peer}, device_id_type=MESH)
        return carry

    load_h = pltpu.make_async_copy(h_hbm, h_ref, local_sem.at[0])
    load_t = pltpu.make_async_copy(t_hbm, t_ref, local_sem.at[1])
    load_x = pltpu.make_async_copy(x_ref.at[w], xs.at[:, w], local_sem.at[2])
    load_place = pltpu.make_async_copy(place_hbm, place_ref, local_sem.at[3])
    load_offset = pltpu.make_async_copy(offset_hbm, offset_ref, local_sem.at[4])
    load_place.start()
    load_offset.start()
    load_h.start()
    load_t.start()
    load_x.start()
    lax.fori_loop(1, n_wide, greet, 0)
    load_place.wait()
    load_offset.wait()
    load_h.wait()

    places = [place_ref[s] for s in range(STEPS)]
    channel, taken = [], 2
    for place in places:
        end = jnp.where(place == slots * n_row - 1, 1, taken)
        channel.append(jnp.where(place == 0, 0, end))
        taken = taken + jnp.where((place == 0) | (place == slots * n_row - 1), 0, 1)

    def of_channel(c, values):
        return sum(jnp.where(channel[s] == c, values[s], 0) for s in range(STEPS))

    starts = [offset_ref[s] for s in range(STEPS)]
    lane = lax.broadcasted_iota(jnp.int32, (BW, SLAB), 1) + w * (slabs * SLAB)
    ends = ((0, 0, 0), (1, n_row - 1, slots - 1))
    half = slabs // 2
    for c, home, slot in ends:
        @pl.when(r == home)
        def _(c=c, slot=slot):
            start = of_channel(c, starts)
            for m in range(half):
                for held, first in ((mine_v, q * half), (other_v, (1 - q) * half)):
                    at = pl.multiple_of((first + m) * SLAB, SLAB)
                    block = h_ref[slot, :, pl.ds(at, SLAB)]
                    held[m, c] = jnp.where(lane + at >= start, block, 0.0)

    for c in range(FREE):
        place = of_channel(2 + c, places)
        start = jnp.where(lax.div(place, slots) == r, of_channel(2 + c, starts), n_wide * slabs * SLAB)
        slot = lax.rem(place, slots)
        for k in range(slabs):
            block = h_ref[slot, :, k * SLAB:(k + 1) * SLAB]
            own[pl.ds((k * FREE + c) * BW, BW)] = jnp.where(lane + k * SLAB >= start, block, 0.0)

    pl.semaphore_wait(barrier, n_wide + 3)

    def copy(src, dst, send, recv, to):
        return pltpu.make_async_remote_copy(
            src_ref=src, dst_ref=dst, send_sem=send, recv_sem=recv, device_id=to, device_id_type=MESH)

    def span(start, size):
        return pl.ds(pl.multiple_of(start, 8), size)

    def send_feed(t):
        for to, odd in ((near, 0), (far, 1)):
            i = lax.div(to, 2) - t + pieces
            i = i + lax.rem(i + odd, 2) * (1 + 2 * t)
            for line in range(LINES):
                for at, size, n in chunks_of(lax.rem(i + line * (pieces // LINES), pieces), isinstance(t, int) and t == 0):
                    copy(own.at[span(other + at, size)], feed.at[span(at, size)], send_sem.at[0], feed_sem.at[n],
                         {"row": to}).start()

    def chunks_of(i, single):
        return [(i * PIECE + j * CHUNK, CHUNK, i * CUTS + j) for j in range(CUTS)] if single else [(i * PIECE, PIECE, i * CUTS)]

    def send_x(d):
        peer = lax.rem(w + d, n_wide)
        copy(x_ref.at[peer], xs.at[:, w], send_sem.at[2], x_sem, {"wide": peer}).start()

    def hop(t, d, line, at, j):
        buf = flow.at[d, line, span(at, CHUNK)]
        return copy(buf, buf, send_sem.at[1], flow_sem.at[d, line, (t + 1) * CUTS + j], {"row": row(2 - 4 * d)})

    def piece(t, d, line):
        return lax.rem(a - t + d * (1 + 2 * t) + line * (pieces // LINES) + pieces, pieces)

    def send_finished(t, d, line):
        i = piece(t, d, line)
        to = near + lax.rem(i, 2) * (far - near)
        m = lax.div(i, 2)
        for j in range(CUTS):
            at, c = i * PIECE + j * CHUNK, 2 + lax.rem(i, 2) * CUTS + j
            here, flowed = span(mine + at, CHUNK), span(at, CHUNK)
            mine_v[m, c] = flow[0, line, flowed] + flow[1, line, flowed] - own[here]
            copy(mine_v.at[m, c], other_v.at[m, c], send_sem.at[5], done_sem, {"row": to}).start()

    def add_feed(t, d, line, single):
        for at, size, n in chunks_of(piece(t, d, line), single):
            here, fed = span(mine + at, size), span(at, size)
            copy(own.at[here], feed.at[fed], send_sem.at[0], feed_sem.at[n], {"row": near}).wait_recv()
            own[here] = own[here] + feed[fed]

    def advance(t, d, line, first=False, last=False):
        for j in range(CUTS):
            at = piece(t, d, line) * PIECE + j * CHUNK
            here, flowed = span(mine + at, CHUNK), span(at, CHUNK)
            if first:
                flow[d, line, flowed] = own[here]
            else:
                hop(t - 1, d, line, at, j).wait_recv()
                flow[d, line, flowed] = flow[d, line, flowed] + own[here]
            if not last:
                hop(t, d, line, at, j).start()

    def first_stream(t):
        crossed_right = lax.div(r + 2 * n_row, CUBE) - lax.div(r + 2 * n_row - 2 * t, CUBE)
        crossed_left = lax.div(r + 2 * t, CUBE) - lax.div(r, CUBE)
        return lax.div(crossed_right - crossed_left + 1, 2)

    def spread(t):
        share = n_wide * 2 // pieces
        lax.fori_loop(t * share, (t + 1) * share, lambda d, c: (send_x(d), c)[1], 0)

    def fixed(c, home, m):
        root = home // 2
        ahead, behind = lax.rem(a - root + pieces, pieces), lax.rem(root - a + pieces, pieces)
        held = mine_v.at[m, c]

        def to(row_at, source, target, sem):
            return copy(source.at[m, c], target.at[m, c], send_sem.at[8], sem, {"row": row_at})

        start = to(near, other_v, mine_v, fixed_sem.at[c, m])
        return jnp.minimum(ahead, behind), start, (
            (ahead < half, to(row(2), mine_v, mine_v, fixed_sem.at[c, m])),
            (behind < half - 1, to(row(-2), mine_v, mine_v, fixed_sem.at[c, m])),
            (near != home, to(near, mine_v, other_v, fixed_done_sem.at[c])))

    def start_fixed():
        for c, home, slot in ends:
            @pl.when(r == home)
            def _(c=c, home=home):
                for m in range(half):
                    fixed(c, home, m)[1].start()

    def pass_fixed(t):
        for c, home, slot in ends:
            root = home // 2
            distance = jnp.minimum(lax.rem(a - root + pieces, pieces), lax.rem(root - a + pieces, pieces))
            m = t - LAG - distance

            @pl.when((m >= 0) & (m < half))
            def _(c=c, home=home, m=m):
                distance, start, onward = fixed(c, home, m)
                pl.when(r != home)(start.wait_recv)
                for wanted, move in onward:
                    pl.when(wanted)(move.start)

    def step(t, last=False):
        d = first_stream(t)
        for d in (d, 1 - d):
            for line in range(LINES):
                advance(t, d, line, last=last)

    feeds = half // LINES

    def feed_in(t, single):
        for d in range(2):
            for line in range(LINES):
                add_feed(t, d, line, single)

    def middle(t, carry):
        pl.when(t < feeds)(lambda: feed_in(t, False))
        step(t)
        pass_fixed(t)
        pl.when(t < feeds - 2)(lambda: send_feed(t + 2))
        spread(t)
        return carry

    send_feed(0)
    start_fixed()
    send_feed(1)
    for d in range(2):
        for line in range(LINES):
            add_feed(0, d, line, True)
            advance(0, d, line, first=True)
    if feeds > 2:
        send_feed(2)
    for d in range(1, n_wide * 2 // pieces):
        send_x(d)
    lax.fori_loop(1, half, middle, 0)
    hops = half + half // LINES - 1
    for t in range(half, hops + 1):
        step(t, last=t == hops)
        for d in range(2):
            for line in range(LINES):
                send_finished(t, d, line)
        pass_fixed(t)
    for t in range(hops + 1, 2 * half + LAG):
        pass_fixed(t)

    def total_of(buf, send, recv, count):
        return copy(buf.at[pl.ds(0, count)], buf.at[pl.ds(0, count)], send, recv, {"row": near})

    load_t.wait()
    diag[...] = jnp.zeros_like(diag)
    for s in range(STEPS):
        at = s * BW % SLAB
        diag[s * BW // SLAB, at:at + BW, at:at + BW] = t_ref[s]
    load_x.wait()
    others = n_wide - 1
    other_x = copy(x_ref.at[pl.ds(0, others)], xs.at[:, pl.ds(0, others)], send_sem.at[2], x_sem, {"row": near})
    other_x.wait_recv()
    x_rows = xs.shape[1] * xs.shape[2]
    all_done = total_of(own, send_sem.at[5], done_sem, side)

    def pair_v(held, m):
        return jnp.concatenate(
            [jnp.concatenate([held[k, channel[s]] for s in range(STEPS)], axis=0) for k in (m, m + 1)], axis=1)

    def pair_x(k):
        return jnp.concatenate([xs[k].reshape(x_rows, SLAB), xs[k + 1].reshape(x_rows, SLAB)], axis=1)

    sides = ((mine_v, q * half), (other_v, (1 - q) * half))

    def products(held, first):
        acc = None
        for m in range(0, half, 2):
            v, x = pair_v(held, m), pair_x(first + m)
            product = dot_t(jnp.concatenate([x, v], axis=0), v)
            acc = product if acc is None else acc + product
        return acc

    acc = products(*sides[0])
    all_done.wait_recv()
    for c, home, slot in ends:
        pl.when(r != home)(copy(mine_v.at[:, c], other_v.at[:, c], send_sem.at[8], fixed_done_sem.at[c],
                                {"row": near}).wait_recv)
    acc = acc + products(*sides[1])

    wide = 2 * SLAB
    padded = jnp.concatenate([acc, jnp.zeros((acc.shape[0], wide - acc.shape[1]), jnp.float32)], axis=1)
    first_gram = x_rows // 8
    core = lax.rem(w, 2)
    chip = lax.div(w, 2)
    twin = w + 1 - 2 * core
    chips = n_wide // 2
    for i in range(chips):
        for c in range(2):
            part[c, i, 0] = padded[i * 8:(i + 1) * 8, c * SLAB:(c + 1) * SLAB]
            tile, column = GRAM_TILES[2 * i + c]
            tile = tile + first_gram
            part[c, i, 1] = padded[tile * 8:(tile + 1) * 8, column * SLAB:(column + 1) * SLAB]

    to_twin = copy(part.at[1 - core], core_in, send_sem.at[6], core_sem.at[0], {"wide": twin})
    to_twin.start()
    to_twin.wait_recv()
    pair[...] = part[core] + core_in[...]

    around = sorted(((dx, dy) for dx in range(4) for dy in range(4) if dx or dy),
                    key=lambda at: -min(at[0], 4 - at[0]) - min(at[1], 4 - at[1]))

    def chip_at(dx, dy):
        return lax.rem(lax.div(chip, 4) + dx, 4) * 4 + lax.rem(lax.rem(chip, 4) + dy, 4)

    for dx, dy in around:
        to = chip_at(dx, dy)
        copy(pair.at[to], gather_in.at[chip], send_sem.at[3], red_sem, {"wide": 2 * to + core}).start()
    gather_in[chip] = pair[chip]
    parts_in = total_of(gather_in, send_sem.at[3], red_sem, chips - 1)
    parts_in.wait_recv()
    total[...] = jnp.sum(gather_in[...], axis=0)

    for dx, dy in around:
        to = chip_at(dx, dy)
        copy(total, gathered.at[core, chip], send_sem.at[4], all_sem, {"wide": 2 * to + core}).start()
    gathered[core, chip] = total[...]
    totals_in = total_of(gather_in, send_sem.at[4], all_sem, chips - 1)
    totals_in.wait_recv()
    all_to_twin = copy(gathered.at[core], gathered.at[core], send_sem.at[7], core_sem.at[1], {"wide": twin})
    all_to_twin.start()
    all_to_twin.wait_recv()

    solved = []
    for c in range(2):
        rows = [gathered[c, i, 0] for i in range(chips)]
        rows += [gathered[i % 2, i // 2, 1] for i in range(n_wide) if GRAM_TILES[i][1] == c]
        solved.append(dot_t(jnp.concatenate(rows, axis=0), diag[c]))
    scaled = []
    for s in range(STEPS):
        c, at = s * BW // SLAB, s * BW % SLAB
        value = solved[c][:x_rows, at:at + BW]
        if s:
            value = value - dot(jnp.concatenate(scaled, axis=1), solved[c][x_rows:x_rows + s * BW, at:at + BW])
        scaled.append(value)
    u = jnp.concatenate(scaled, axis=1)
    for held, first in sides:
        for m in range(0, half, 2):
            at = pl.multiple_of((first + m) * SLAB, 2 * SLAB)
            out_ref[:, pl.ds(at, 2 * SLAB)] = pair_x(first + m) - dot(u, pair_v(held, m))

    total_of(own, send_sem.at[0], feed_sem.at[0], side).wait_send()
    flowed = flow.at[:, :, pl.ds(0, hops * PIECE)]
    copy(flowed, flowed, send_sem.at[1], feed_sem.at[0], {"row": near}).wait_send()
    for c, home, slot in ends:
        for m in range(half):
            distance, start, onward = fixed(c, home, m)
            pl.when(r == home)(start.wait_send)
            for wanted, move in onward:
                pl.when(wanted)(move.wait_send)
    other_x.wait_send()
    all_done.wait_send()
    parts_in.wait_send()
    totals_in.wait_send()
    to_twin.wait_send()
    all_to_twin.wait_send()


def body(n_row, n_wide, eigvec_t, householder, wy_factor, block_place, offsets):
    local = eigvec_t.shape[0]
    ncols = householder.shape[2]
    slabs = ncols // SLAB
    side = slabs * PIECE
    x = eigvec_t.reshape(local, n_wide, slabs, SLAB).transpose(1, 2, 0, 3)
    chips = n_wide // 2
    hbm = pl.BlockSpec(memory_space=pltpu.HBM)
    operands = [pltpu.with_memory_space_constraint(v, pltpu.HBM)
                for v in (block_place, offsets, x, householder, wy_factor)]
    f32 = jnp.float32
    return pl.pallas_call(
        functools.partial(kernel, n_row, n_wide),
        out_shape=jax.ShapeDtypeStruct((local * n_wide, ncols), f32),
        in_specs=[hbm] * 5,
        out_specs=pl.BlockSpec(memory_space=pltpu.VMEM),
        scratch_shapes=[
            pltpu.SMEM(block_place.shape, jnp.int32),
            pltpu.SMEM(offsets.shape, jnp.int32),
            pltpu.VMEM(householder.shape, f32),
            pltpu.VMEM(wy_factor.shape, f32),
            pltpu.VMEM((2, SLAB, SLAB), f32),
            pltpu.VMEM((2 * side, SLAB), f32),
            pltpu.VMEM((side, SLAB), f32),
            pltpu.VMEM((2, LINES, side, SLAB), f32),
            pltpu.VMEM((slabs // 2, STEPS, BW, SLAB), f32),
            pltpu.VMEM((slabs // 2, STEPS, BW, SLAB), f32),
            pltpu.VMEM((slabs, n_wide, local, SLAB), f32),
            pltpu.VMEM((2, chips, 2, 8, SLAB), f32),
            pltpu.VMEM((chips, 2, 8, SLAB), f32),
            pltpu.VMEM((chips, 2, 8, SLAB), f32),
            pltpu.VMEM((chips, 2, 8, SLAB), f32),
            pltpu.VMEM((2, 8, SLAB), f32),
            pltpu.VMEM((2, chips, 2, 8, SLAB), f32),
            pltpu.SemaphoreType.DMA((slabs * CUTS,)),
            pltpu.SemaphoreType.DMA((2, LINES, slabs * CUTS)),
            pltpu.SemaphoreType.DMA,
            pltpu.SemaphoreType.DMA((2, slabs // 2)),
            pltpu.SemaphoreType.DMA((2,)),
            pltpu.SemaphoreType.DMA,
            pltpu.SemaphoreType.DMA((2,)),
            pltpu.SemaphoreType.DMA,
            pltpu.SemaphoreType.DMA,
            pltpu.SemaphoreType.DMA((9,)),
            pltpu.SemaphoreType.DMA((5,)),
        ],
        compiler_params=pltpu.CompilerParams(collective_id=0, has_side_effects=True, vmem_limit_bytes=32 << 20),
    )(*operands)


def solution(mesh):
    n_row, n_wide = mesh.shape["row"], mesh.shape["wide"]
    return jax.shard_map(
        functools.partial(body, n_row, n_wide),
        mesh=mesh,
        in_specs=(P(("row", "wide"), None), P("row", None, "wide"), P(), P(), P()),
        out_specs=P("row", "wide"),
        check_vma=False,
    )
```

```python
import functools

import jax
import jax.numpy as jnp
from jax import lax
from jax.experimental import pallas as pl
from jax.experimental.pallas import tpu as pltpu
from jax.sharding import PartitionSpec as P

MESH = pl.DeviceIdType.MESH
STEPS, BW, SLAB, CUBE = 6, 32, 128, 4
FREE = STEPS - 2
CUTS = FREE // 2
LINES, LAG, GROUP = 2, 1, 2
PIECE = CUTS * BW
CHUNK = BW
GRAM_TILES = [(i, 0) for i in range(12)] + [(i, 1) for i in range(20)]


def split(a):
    high = a.astype(jnp.bfloat16)
    return high, (a - high.astype(jnp.float32)).astype(jnp.bfloat16)


def contract(a, b, dims):
    (a1, a2), (b1, b2) = split(a), split(b)

    def one(x, y):
        return lax.dot_general(x, y, (dims, ((), ())), preferred_element_type=jnp.float32)

    return one(a1, b1) + (one(a1, b2) + one(a2, b1))


def exact(a, b, dims):
    return lax.dot_general(a, b, (dims, ((), ())), precision=lax.Precision.HIGHEST, preferred_element_type=jnp.float32)


def dot_t(a, b):
    return contract(a, b, ((1,), (1,)))


def dot(a, b):
    return contract(a, b, ((1,), (0,)))


def kernel(n_row, n_wide, place_hbm, offset_hbm, x_ref, h_hbm, t_hbm, out_ref,
           place_ref, offset_ref, h_ref, t_ref, diag, own, feed, flow, mine_v, other_v, xs,
           part, core_in, pair, gather_in, total, gathered,
           feed_sem, flow_sem, done_sem, fixed_sem, fixed_done_sem, x_sem, core_sem, red_sem, all_sem, send_sem, local_sem):
    r = lax.axis_index("row")
    w = lax.axis_index("wide")
    slots = h_ref.shape[0]
    slabs = h_ref.shape[2] // SLAB
    pieces = slabs
    side = pieces * PIECE
    q = lax.rem(r, 2)
    a = lax.div(r, 2)
    mine, other = q * side, (1 - q) * side

    def row(delta):
        return lax.rem(r + delta + n_row, n_row)

    near, far = row(1 - 2 * q), row(2 * q - 1)

    barrier = pltpu.get_barrier_semaphore()
    for delta in (1, -1, 2, -2):
        pl.semaphore_signal(barrier, inc=1, device_id={"row": row(delta)}, device_id_type=MESH)

    def greet(d, carry):
        peer = lax.rem(w + d, n_wide)
        pl.semaphore_signal(barrier, inc=1, device_id={"wide": peer}, device_id_type=MESH)
        return carry

    load_h = pltpu.make_async_copy(h_hbm, h_ref, local_sem.at[0])
    load_t = pltpu.make_async_copy(t_hbm, t_ref, local_sem.at[1])
    load_x = pltpu.make_async_copy(x_ref.at[w], xs.at[:, w], local_sem.at[2])
    load_place = pltpu.make_async_copy(place_hbm, place_ref, local_sem.at[3])
    load_offset = pltpu.make_async_copy(offset_hbm, offset_ref, local_sem.at[4])
    load_place.start()
    load_offset.start()
    load_h.start()
    load_t.start()
    load_x.start()
    lax.fori_loop(1, n_wide, greet, 0)
    load_place.wait()
    load_offset.wait()
    load_h.wait()

    places = [place_ref[s] for s in range(STEPS)]
    channel, taken = [], 2
    for place in places:
        end = jnp.where(place == slots * n_row - 1, 1, taken)
        channel.append(jnp.where(place == 0, 0, end))
        taken = taken + jnp.where((place == 0) | (place == slots * n_row - 1), 0, 1)

    def of_channel(c, values):
        return sum(jnp.where(channel[s] == c, values[s], 0) for s in range(STEPS))

    starts = [offset_ref[s] for s in range(STEPS)]
    lane = lax.broadcasted_iota(jnp.int32, (BW, SLAB), 1) + w * (slabs * SLAB)
    ends = ((0, 0, 0), (1, n_row - 1, slots - 1))
    half = slabs // 2
    free = []
    for c in range(FREE):
        place = of_channel(2 + c, places)
        start = jnp.where(lax.div(place, slots) == r, of_channel(2 + c, starts), n_wide * slabs * SLAB)
        free.append((lax.rem(place, slots), start))

    def stage(first):
        for m in range(half):
            at = pl.multiple_of((first + m) * SLAB, SLAB)
            for c, (slot, start) in enumerate(free):
                block = h_ref[slot, :, pl.ds(at, SLAB)]
                own[pl.ds(((first + m) * FREE + c) * BW, BW)] = jnp.where(lane + at >= start, block, 0.0)

    stage((1 - q) * half)
    pl.semaphore_wait(barrier, n_wide + 3)

    def copy(src, dst, send, recv, to):
        return pltpu.make_async_remote_copy(
            src_ref=src, dst_ref=dst, send_sem=send, recv_sem=recv, device_id=to, device_id_type=MESH)

    def span(start, size):
        return pl.ds(pl.multiple_of(start, 8), size)

    def send_feed(t):
        for to, odd in ((near, 0), (far, 1)):
            i = lax.div(to, 2) - t + pieces
            i = i + lax.rem(i + odd, 2) * (1 + 2 * t)
            for line in range(LINES):
                for at, size, n in chunks_of(lax.rem(i + line * (pieces // LINES), pieces), isinstance(t, int) and t == 0):
                    copy(own.at[span(other + at, size)], feed.at[span(at, size)], send_sem.at[0], feed_sem.at[n],
                         {"row": to}).start()

    def chunks_of(i, single):
        return [(i * PIECE + j * CHUNK, CHUNK, i * CUTS + j) for j in range(CUTS)] if single else [(i * PIECE, PIECE, i * CUTS)]

    def send_x(d):
        peer = lax.rem(w + d, n_wide)
        copy(x_ref.at[peer], xs.at[:, w], send_sem.at[2], x_sem, {"wide": peer}).start()

    def hop(t, d, line, at, j):
        buf = flow.at[d, line, span(at, CHUNK)]
        return copy(buf, buf, send_sem.at[1], flow_sem.at[d, line, (t + 1) * CUTS + j], {"row": row(2 - 4 * d)})

    def piece(t, d, line):
        return lax.rem(a - t + d * (1 + 2 * t) + line * (pieces // LINES) + pieces, pieces)

    def send_finished(t, d, line):
        i = piece(t, d, line)
        to = near + lax.rem(i, 2) * (far - near)
        m = lax.div(i, 2)
        for j in range(CUTS):
            at, c = i * PIECE + j * CHUNK, 2 + lax.rem(i, 2) * CUTS + j
            here, flowed = span(mine + at, CHUNK), span(at, CHUNK)
            mine_v[m, c] = flow[0, line, flowed] + flow[1, line, flowed] - own[here]
            copy(mine_v.at[m, c], other_v.at[m, c], send_sem.at[5], done_sem, {"row": to}).start()

    def add_feed(t, d, line, single):
        for at, size, n in chunks_of(piece(t, d, line), single):
            here, fed = span(mine + at, size), span(at, size)
            copy(own.at[here], feed.at[fed], send_sem.at[0], feed_sem.at[n], {"row": near}).wait_recv()
            own[here] = own[here] + feed[fed]

    def advance(t, d, line, first=False, last=False):
        for j in range(CUTS):
            at = piece(t, d, line) * PIECE + j * CHUNK
            here, flowed = span(mine + at, CHUNK), span(at, CHUNK)
            if first:
                flow[d, line, flowed] = own[here]
            else:
                hop(t - 1, d, line, at, j).wait_recv()
                flow[d, line, flowed] = flow[d, line, flowed] + own[here]
            if not last:
                hop(t, d, line, at, j).start()

    def first_stream(t):
        crossed_right = lax.div(r + 2 * n_row, CUBE) - lax.div(r + 2 * n_row - 2 * t, CUBE)
        crossed_left = lax.div(r + 2 * t, CUBE) - lax.div(r, CUBE)
        return lax.div(crossed_right - crossed_left + 1, 2)

    def spread(t):
        share = n_wide * 2 // pieces
        lax.fori_loop(t * share, (t + 1) * share, lambda d, c: (send_x(d), c)[1], 0)

    def fixed(c, home, m):
        root = home // 2
        ahead, behind = lax.rem(a - root + pieces, pieces), lax.rem(root - a + pieces, pieces)
        held = mine_v.at[m, c]

        def to(row_at, source, target, sem):
            return copy(source.at[m, c], target.at[m, c], send_sem.at[8], sem, {"row": row_at})

        start = to(near, other_v, mine_v, fixed_sem.at[c, m])
        return jnp.minimum(ahead, behind), start, (
            (ahead < half, to(row(2), mine_v, mine_v, fixed_sem.at[c, m])),
            (behind < half - 1, to(row(-2), mine_v, mine_v, fixed_sem.at[c, m])),
            (near != home, to(near, mine_v, other_v, fixed_done_sem.at[c])))

    def start_fixed():
        for c, home, slot in ends:
            @pl.when(r == home)
            def _(c=c, home=home):
                for m in range(half):
                    fixed(c, home, m)[1].start()

    def pass_fixed(t):
        for c, home, slot in ends:
            root = home // 2
            distance = jnp.minimum(lax.rem(a - root + pieces, pieces), lax.rem(root - a + pieces, pieces))
            turn = t - LAG - distance

            @pl.when((turn >= 0) & (turn < half // GROUP))
            def _(c=c, home=home, turn=turn):
                for m in range(GROUP):
                    distance, start, onward = fixed(c, home, turn * GROUP + m)
                    pl.when(r != home)(start.wait_recv)
                    for wanted, move in onward:
                        pl.when(wanted)(move.start)

    def step(t, last=False):
        d = first_stream(t)
        for d in (d, 1 - d):
            for line in range(LINES):
                advance(t, d, line, last=last)

    feeds = half // LINES

    def feed_in(t, single):
        for d in range(2):
            for line in range(LINES):
                add_feed(t, d, line, single)

    def middle(t, carry):
        pl.when(t < feeds)(lambda: feed_in(t, False))
        step(t)
        pass_fixed(t)
        pl.when(t < feeds - 2)(lambda: send_feed(t + 2))
        spread(t)
        return carry

    send_feed(0)
    for c, home, slot in ends:
        @pl.when(r == home)
        def _(c=c, slot=slot):
            start = of_channel(c, starts)
            for m in range(half):
                for held, first in ((mine_v, q * half), (other_v, (1 - q) * half)):
                    at = pl.multiple_of((first + m) * SLAB, SLAB)
                    block = h_ref[slot, :, pl.ds(at, SLAB)]
                    held[m, c] = jnp.where(lane + at >= start, block, 0.0)
    start_fixed()
    send_feed(1)
    stage(q * half)
    for d in range(2):
        for line in range(LINES):
            add_feed(0, d, line, True)
            advance(0, d, line, first=True)
    if feeds > 2:
        send_feed(2)
    for d in range(1, n_wide * 2 // pieces):
        send_x(d)
    lax.fori_loop(1, half, middle, 0)
    hops = half + half // LINES - 1
    for t in range(half, hops + 1):
        step(t, last=t == hops)
        for d in range(2):
            for line in range(LINES):
                send_finished(t, d, line)
        pass_fixed(t)
    for t in range(hops + 1, half + half // GROUP + LAG):
        pass_fixed(t)

    def total_of(buf, send, recv, count):
        return copy(buf.at[pl.ds(0, count)], buf.at[pl.ds(0, count)], send, recv, {"row": near})

    load_t.wait()
    diag[...] = jnp.zeros_like(diag)
    for s in range(STEPS):
        at = s * BW % SLAB
        diag[s * BW // SLAB, at:at + BW, at:at + BW] = t_ref[s]
    load_x.wait()
    others = n_wide - 1
    other_x = copy(x_ref.at[pl.ds(0, others)], xs.at[:, pl.ds(0, others)], send_sem.at[2], x_sem, {"row": near})
    other_x.wait_recv()
    x_rows = xs.shape[1] * xs.shape[2]
    all_done = total_of(own, send_sem.at[5], done_sem, side)

    def pair_v(held, m):
        return jnp.concatenate(
            [jnp.concatenate([held[k, channel[s]] for s in range(STEPS)], axis=0) for k in (m, m + 1)], axis=1)

    def pair_x(k):
        return jnp.concatenate([xs[k].reshape(x_rows, SLAB), xs[k + 1].reshape(x_rows, SLAB)], axis=1)

    sides = ((mine_v, q * half), (other_v, (1 - q) * half))

    def products(held, first):
        acc = None
        for m in range(0, half, 2):
            v, x = pair_v(held, m), pair_x(first + m)
            product = dot_t(jnp.concatenate([x, v], axis=0), v)
            acc = product if acc is None else acc + product
        return acc

    acc = products(*sides[0])
    all_done.wait_recv()
    for c, home, slot in ends:
        pl.when(r != home)(copy(mine_v.at[:, c], other_v.at[:, c], send_sem.at[8], fixed_done_sem.at[c],
                                {"row": near}).wait_recv)
    acc = acc + products(*sides[1])

    wide = 2 * SLAB
    padded = jnp.concatenate([acc, jnp.zeros((acc.shape[0], wide - acc.shape[1]), jnp.float32)], axis=1)
    first_gram = x_rows // 8
    core = lax.rem(w, 2)
    chip = lax.div(w, 2)
    twin = w + 1 - 2 * core
    chips = n_wide // 2
    for i in range(chips):
        for c in range(2):
            part[c, i, 0] = padded[i * 8:(i + 1) * 8, c * SLAB:(c + 1) * SLAB]
            tile, column = GRAM_TILES[2 * i + c]
            tile = tile + first_gram
            part[c, i, 1] = padded[tile * 8:(tile + 1) * 8, column * SLAB:(column + 1) * SLAB]

    to_twin = copy(part.at[1 - core], core_in, send_sem.at[6], core_sem.at[0], {"wide": twin})
    to_twin.start()
    to_twin.wait_recv()
    pair[...] = part[core] + core_in[...]

    around = sorted(((dx, dy) for dx in range(4) for dy in range(4) if dx or dy),
                    key=lambda at: -min(at[0], 4 - at[0]) - min(at[1], 4 - at[1]))

    def chip_at(dx, dy):
        return lax.rem(lax.div(chip, 4) + dx, 4) * 4 + lax.rem(lax.rem(chip, 4) + dy, 4)

    for dx, dy in around:
        to = chip_at(dx, dy)
        copy(pair.at[to], gather_in.at[chip], send_sem.at[3], red_sem, {"wide": 2 * to + core}).start()
    gather_in[chip] = pair[chip]
    parts_in = total_of(gather_in, send_sem.at[3], red_sem, chips - 1)
    parts_in.wait_recv()
    total[...] = jnp.sum(gather_in[...], axis=0)

    for dx, dy in around:
        to = chip_at(dx, dy)
        copy(total, gathered.at[core, chip], send_sem.at[4], all_sem, {"wide": 2 * to + core}).start()
    gathered[core, chip] = total[...]
    totals_in = total_of(gather_in, send_sem.at[4], all_sem, chips - 1)
    totals_in.wait_recv()
    all_to_twin = copy(gathered.at[core], gathered.at[core], send_sem.at[7], core_sem.at[1], {"wide": twin})
    all_to_twin.start()
    all_to_twin.wait_recv()

    solved = []
    for c in range(2):
        rows = [gathered[c, i, 0] for i in range(chips)]
        rows += [gathered[i % 2, i // 2, 1] for i in range(n_wide) if GRAM_TILES[i][1] == c]
        solved.append(exact(jnp.concatenate(rows, axis=0), diag[c], ((1,), (1,))))
    scaled = []
    for s in range(STEPS):
        c, at = s * BW // SLAB, s * BW % SLAB
        value = solved[c][:x_rows, at:at + BW]
        if s:
            overlap = solved[c][x_rows:x_rows + s * BW, at:at + BW]
            value = value - exact(jnp.concatenate(scaled, axis=1), overlap, ((1,), (0,)))
        scaled.append(value)
    u = jnp.concatenate(scaled, axis=1)
    for held, first in sides:
        for m in range(0, half, 2):
            at = pl.multiple_of((first + m) * SLAB, 2 * SLAB)
            out_ref[:, pl.ds(at, 2 * SLAB)] = pair_x(first + m) - dot(u, pair_v(held, m))

    total_of(own, send_sem.at[0], feed_sem.at[0], side).wait_send()
    flowed = flow.at[:, :, pl.ds(0, hops * PIECE)]
    copy(flowed, flowed, send_sem.at[1], feed_sem.at[0], {"row": near}).wait_send()
    for c, home, slot in ends:
        for m in range(half):
            distance, start, onward = fixed(c, home, m)
            pl.when(r == home)(start.wait_send)
            for wanted, move in onward:
                pl.when(wanted)(move.wait_send)
    other_x.wait_send()
    all_done.wait_send()
    parts_in.wait_send()
    totals_in.wait_send()
    to_twin.wait_send()
    all_to_twin.wait_send()


def body(n_row, n_wide, eigvec_t, householder, wy_factor, block_place, offsets):
    local = eigvec_t.shape[0]
    ncols = householder.shape[2]
    slabs = ncols // SLAB
    side = slabs * PIECE
    x = eigvec_t.reshape(local, n_wide, slabs, SLAB).transpose(1, 2, 0, 3)
    chips = n_wide // 2
    hbm = pl.BlockSpec(memory_space=pltpu.HBM)
    operands = [pltpu.with_memory_space_constraint(v, pltpu.HBM)
                for v in (block_place, offsets, x, householder, wy_factor)]
    f32 = jnp.float32
    return pl.pallas_call(
        functools.partial(kernel, n_row, n_wide),
        out_shape=jax.ShapeDtypeStruct((local * n_wide, ncols), f32),
        in_specs=[hbm] * 5,
        out_specs=pl.BlockSpec(memory_space=pltpu.VMEM),
        scratch_shapes=[
            pltpu.SMEM(block_place.shape, jnp.int32),
            pltpu.SMEM(offsets.shape, jnp.int32),
            pltpu.VMEM(householder.shape, f32),
            pltpu.VMEM(wy_factor.shape, f32),
            pltpu.VMEM((2, SLAB, SLAB), f32),
            pltpu.VMEM((2 * side, SLAB), f32),
            pltpu.VMEM((side, SLAB), f32),
            pltpu.VMEM((2, LINES, side, SLAB), f32),
            pltpu.VMEM((slabs // 2, STEPS, BW, SLAB), f32),
            pltpu.VMEM((slabs // 2, STEPS, BW, SLAB), f32),
            pltpu.VMEM((slabs, n_wide, local, SLAB), f32),
            pltpu.VMEM((2, chips, 2, 8, SLAB), f32),
            pltpu.VMEM((chips, 2, 8, SLAB), f32),
            pltpu.VMEM((chips, 2, 8, SLAB), f32),
            pltpu.VMEM((chips, 2, 8, SLAB), f32),
            pltpu.VMEM((2, 8, SLAB), f32),
            pltpu.VMEM((2, chips, 2, 8, SLAB), f32),
            pltpu.SemaphoreType.DMA((slabs * CUTS,)),
            pltpu.SemaphoreType.DMA((2, LINES, slabs * CUTS)),
            pltpu.SemaphoreType.DMA,
            pltpu.SemaphoreType.DMA((2, slabs // 2)),
            pltpu.SemaphoreType.DMA((2,)),
            pltpu.SemaphoreType.DMA,
            pltpu.SemaphoreType.DMA((2,)),
            pltpu.SemaphoreType.DMA,
            pltpu.SemaphoreType.DMA,
            pltpu.SemaphoreType.DMA((9,)),
            pltpu.SemaphoreType.DMA((5,)),
        ],
        compiler_params=pltpu.CompilerParams(collective_id=0, has_side_effects=True, vmem_limit_bytes=32 << 20),
    )(*operands)


def solution(mesh):
    n_row, n_wide = mesh.shape["row"], mesh.shape["wide"]
    return jax.shard_map(
        functools.partial(body, n_row, n_wide),
        mesh=mesh,
        in_specs=(P(("row", "wide"), None), P("row", None, "wide"), P(), P(), P()),
        out_specs=P("row", "wide"),
        check_vma=False,
    )
```

```python
import functools

import jax
import jax.numpy as jnp
from jax import lax
from jax.experimental import pallas as pl
from jax.experimental.pallas import tpu as pltpu
from jax.sharding import PartitionSpec as P

MESH = pl.DeviceIdType.MESH
STEPS, BW, SLAB, CUBE = 6, 32, 128, 4
FREE = STEPS - 2
CUTS = FREE // 2
LINES, LAG, GROUP = 2, 1, 2
PIECE = CUTS * BW
CHUNK = BW
GRAM_TILES = [(i, 0) for i in range(12)] + [(i, 1) for i in range(20)]


def split(a):
    high = a.astype(jnp.bfloat16)
    return high, (a - high.astype(jnp.float32)).astype(jnp.bfloat16)


def contract(a, b, dims):
    (a1, a2), (b1, b2) = a, b

    def one(x, y):
        return lax.dot_general(x, y, (dims, ((), ())), preferred_element_type=jnp.float32)

    return one(a1, b1) + (one(a1, b2) + one(a2, b1))


def dot_t(a, b):
    return contract(a, b, ((1,), (1,)))


def dot(a, b):
    return contract(a, b, ((1,), (0,)))


def kernel(n_row, n_wide, place_hbm, offset_hbm, x_ref, h_hbm, t_hbm, out_ref,
           place_ref, offset_ref, h_ref, t_ref, diag, own, feed, flow, mine_v, other_v, xs,
           part, core_in, pair, gather_in, total, gathered,
           feed_sem, flow_sem, done_sem, fixed_sem, fixed_done_sem, x_sem, core_sem, red_sem, all_sem, send_sem, local_sem):
    r = lax.axis_index("row")
    w = lax.axis_index("wide")
    slots = h_ref.shape[0]
    slabs = h_ref.shape[2] // SLAB
    pieces = slabs
    side = pieces * PIECE
    q = lax.rem(r, 2)
    a = lax.div(r, 2)
    mine, other = q * side, (1 - q) * side

    def row(delta):
        return lax.rem(r + delta + n_row, n_row)

    near, far = row(1 - 2 * q), row(2 * q - 1)

    barrier = pltpu.get_barrier_semaphore()
    for delta in (1, -1, 2, -2):
        pl.semaphore_signal(barrier, inc=1, device_id={"row": row(delta)}, device_id_type=MESH)

    def greet(d, carry):
        peer = lax.rem(w + d, n_wide)
        pl.semaphore_signal(barrier, inc=1, device_id={"wide": peer}, device_id_type=MESH)
        return carry

    load_h = pltpu.make_async_copy(h_hbm, h_ref, local_sem.at[0])
    load_t = pltpu.make_async_copy(t_hbm, t_ref, local_sem.at[1])
    load_x = pltpu.make_async_copy(x_ref.at[w], xs.at[:, w], local_sem.at[2])
    load_place = pltpu.make_async_copy(place_hbm, place_ref, local_sem.at[3])
    load_offset = pltpu.make_async_copy(offset_hbm, offset_ref, local_sem.at[4])
    load_place.start()
    load_offset.start()
    load_h.start()
    load_t.start()
    load_x.start()
    lax.fori_loop(1, n_wide, greet, 0)
    load_place.wait()
    load_offset.wait()
    load_h.wait()

    places = [place_ref[s] for s in range(STEPS)]
    channel, taken = [], 2
    for place in places:
        end = jnp.where(place == slots * n_row - 1, 1, taken)
        channel.append(jnp.where(place == 0, 0, end))
        taken = taken + jnp.where((place == 0) | (place == slots * n_row - 1), 0, 1)

    def of_channel(c, values):
        return sum(jnp.where(channel[s] == c, values[s], 0) for s in range(STEPS))

    starts = [offset_ref[s] for s in range(STEPS)]
    lane = lax.broadcasted_iota(jnp.int32, (BW, SLAB), 1) + w * (slabs * SLAB)
    ends = ((0, 0, 0), (1, n_row - 1, slots - 1))
    half = slabs // 2
    free = []
    for c in range(FREE):
        place = of_channel(2 + c, places)
        start = jnp.where(lax.div(place, slots) == r, of_channel(2 + c, starts), n_wide * slabs * SLAB)
        free.append((lax.rem(place, slots), start))

    def stage(first):
        for m in range(half):
            at = pl.multiple_of((first + m) * SLAB, SLAB)
            for c, (slot, start) in enumerate(free):
                block = h_ref[slot, :, pl.ds(at, SLAB)]
                own[pl.ds(((first + m) * FREE + c) * BW, BW)] = jnp.where(lane + at >= start, block, 0.0)

    stage((1 - q) * half)
    pl.semaphore_wait(barrier, n_wide + 3)

    def copy(src, dst, send, recv, to):
        return pltpu.make_async_remote_copy(
            src_ref=src, dst_ref=dst, send_sem=send, recv_sem=recv, device_id=to, device_id_type=MESH)

    def span(start, size):
        return pl.ds(pl.multiple_of(start, 8), size)

    def send_feed(t):
        for to, odd in ((near, 0), (far, 1)):
            i = lax.div(to, 2) - t + pieces
            i = i + lax.rem(i + odd, 2) * (1 + 2 * t)
            for line in range(LINES):
                for at, size, n in chunks_of(lax.rem(i + line * (pieces // LINES), pieces), isinstance(t, int) and t == 0):
                    copy(own.at[span(other + at, size)], feed.at[span(at, size)], send_sem.at[0], feed_sem.at[n],
                         {"row": to}).start()

    def chunks_of(i, single):
        return [(i * PIECE + j * CHUNK, CHUNK, i * CUTS + j) for j in range(CUTS)] if single else [(i * PIECE, PIECE, i * CUTS)]

    def send_x(d):
        peer = lax.rem(w + d, n_wide)
        copy(x_ref.at[peer], xs.at[:, w], send_sem.at[2], x_sem, {"wide": peer}).start()

    def hop(t, d, line, at, j):
        buf = flow.at[d, line, span(at, CHUNK)]
        return copy(buf, buf, send_sem.at[1], flow_sem.at[d, line, (t + 1) * CUTS + j], {"row": row(2 - 4 * d)})

    def piece(t, d, line):
        return lax.rem(a - t + d * (1 + 2 * t) + line * (pieces // LINES) + pieces, pieces)

    def send_finished(t, d, line):
        i = piece(t, d, line)
        to = near + lax.rem(i, 2) * (far - near)
        m = lax.div(i, 2)
        for j in range(CUTS):
            at, c = i * PIECE + j * CHUNK, 2 + lax.rem(i, 2) * CUTS + j
            here, flowed = span(mine + at, CHUNK), span(at, CHUNK)
            mine_v[m, c] = flow[0, line, flowed] + flow[1, line, flowed] - own[here]
            copy(mine_v.at[m, c], other_v.at[m, c], send_sem.at[5], done_sem, {"row": to}).start()

    def add_feed(t, d, line, single):
        for at, size, n in chunks_of(piece(t, d, line), single):
            here, fed = span(mine + at, size), span(at, size)
            copy(own.at[here], feed.at[fed], send_sem.at[0], feed_sem.at[n], {"row": near}).wait_recv()
            own[here] = own[here] + feed[fed]

    def advance(t, d, line, first=False, last=False):
        for j in range(CUTS):
            at = piece(t, d, line) * PIECE + j * CHUNK
            here, flowed = span(mine + at, CHUNK), span(at, CHUNK)
            if first:
                flow[d, line, flowed] = own[here]
            else:
                hop(t - 1, d, line, at, j).wait_recv()
                flow[d, line, flowed] = flow[d, line, flowed] + own[here]
            if not last:
                hop(t, d, line, at, j).start()

    def first_stream(t):
        crossed_right = lax.div(r + 2 * n_row, CUBE) - lax.div(r + 2 * n_row - 2 * t, CUBE)
        crossed_left = lax.div(r + 2 * t, CUBE) - lax.div(r, CUBE)
        return lax.div(crossed_right - crossed_left + 1, 2)

    def spread(t):
        share = n_wide * 2 // pieces
        lax.fori_loop(t * share, (t + 1) * share, lambda d, c: (send_x(d), c)[1], 0)

    def fixed(c, home, m):
        root = home // 2
        ahead, behind = lax.rem(a - root + pieces, pieces), lax.rem(root - a + pieces, pieces)
        held = mine_v.at[m, c]

        def to(row_at, source, target, sem):
            return copy(source.at[m, c], target.at[m, c], send_sem.at[8], sem, {"row": row_at})

        start = to(near, other_v, mine_v, fixed_sem.at[c, m])
        return jnp.minimum(ahead, behind), start, (
            (ahead < half, to(row(2), mine_v, mine_v, fixed_sem.at[c, m])),
            (behind < half - 1, to(row(-2), mine_v, mine_v, fixed_sem.at[c, m])),
            (near != home, to(near, mine_v, other_v, fixed_done_sem.at[c])))

    def start_fixed():
        for c, home, slot in ends:
            @pl.when(r == home)
            def _(c=c, home=home):
                for m in range(half):
                    fixed(c, home, m)[1].start()

    def pass_fixed(t):
        for c, home, slot in ends:
            root = home // 2
            distance = jnp.minimum(lax.rem(a - root + pieces, pieces), lax.rem(root - a + pieces, pieces))
            turn = t - LAG - distance

            @pl.when((turn >= 0) & (turn < half // GROUP))
            def _(c=c, home=home, turn=turn):
                for m in range(GROUP):
                    distance, start, onward = fixed(c, home, turn * GROUP + m)
                    pl.when(r != home)(start.wait_recv)
                    for wanted, move in onward:
                        pl.when(wanted)(move.start)

    def step(t, last=False):
        d = first_stream(t)
        for line in range(LINES):
            for way in (d, 1 - d):
                advance(t, way, line, last=last)

    feeds = half // LINES

    def feed_in(t, single):
        for d in range(2):
            for line in range(LINES):
                add_feed(t, d, line, single)

    def middle(t, carry):
        pl.when(t < feeds)(lambda: feed_in(t, False))
        step(t)
        pass_fixed(t)
        pl.when(t < feeds - 2)(lambda: send_feed(t + 2))
        spread(t)
        return carry

    send_feed(0)
    for c, home, slot in ends:
        @pl.when(r == home)
        def _(c=c, slot=slot):
            start = of_channel(c, starts)
            for m in range(half):
                for held, first in ((mine_v, q * half), (other_v, (1 - q) * half)):
                    at = pl.multiple_of((first + m) * SLAB, SLAB)
                    block = h_ref[slot, :, pl.ds(at, SLAB)]
                    held[m, c] = jnp.where(lane + at >= start, block, 0.0)
    start_fixed()
    send_feed(1)
    stage(q * half)
    for d in range(2):
        for line in range(LINES):
            add_feed(0, d, line, True)
            advance(0, d, line, first=True)
    if feeds > 2:
        send_feed(2)
    for d in range(1, n_wide * 2 // pieces):
        send_x(d)
    lax.fori_loop(1, half, middle, 0)
    hops = half + half // LINES - 1
    for t in range(half, hops + 1):
        step(t, last=t == hops)
        for line in range(LINES):
            for d in range(2):
                send_finished(t, d, line)
        pass_fixed(t)
    for t in range(hops + 1, half + half // GROUP + LAG):
        pass_fixed(t)

    def total_of(buf, send, recv, count):
        return copy(buf.at[pl.ds(0, count)], buf.at[pl.ds(0, count)], send, recv, {"row": near})

    load_t.wait()
    diag[...] = jnp.zeros_like(diag)
    for s in range(STEPS):
        at = s * BW % SLAB
        diag[s * BW // SLAB, at:at + BW, at:at + BW] = t_ref[s]
    load_x.wait()
    others = n_wide - 1
    other_x = copy(x_ref.at[pl.ds(0, others)], xs.at[:, pl.ds(0, others)], send_sem.at[2], x_sem, {"row": near})
    other_x.wait_recv()
    x_rows = xs.shape[1] * xs.shape[2]
    all_done = total_of(own, send_sem.at[5], done_sem, side)

    def pair_v(held, m):
        return jnp.concatenate(
            [jnp.concatenate([held[k, channel[s]] for s in range(STEPS)], axis=0) for k in (m, m + 1)], axis=1)

    def pair_x(k):
        return jnp.concatenate([xs[k].reshape(x_rows, SLAB), xs[k + 1].reshape(x_rows, SLAB)], axis=1)

    sides = ((mine_v, q * half), (other_v, (1 - q) * half))

    def products(held, first):
        acc = None
        for m in range(0, half, 2):
            v, x = pair_v(held, m), pair_x(first + m)
            v, x = split(v), split(x)
            product = dot_t([jnp.concatenate(both, axis=0) for both in zip(x, v)], v)
            acc = product if acc is None else acc + product
        return acc

    acc = products(*sides[0])
    all_done.wait_recv()
    for c, home, slot in ends:
        pl.when(r != home)(copy(mine_v.at[:, c], other_v.at[:, c], send_sem.at[8], fixed_done_sem.at[c],
                                {"row": near}).wait_recv)
    acc = acc + products(*sides[1])

    wide = 2 * SLAB
    padded = jnp.concatenate([acc, jnp.zeros((acc.shape[0], wide - acc.shape[1]), jnp.float32)], axis=1)
    first_gram = x_rows // 8
    core = lax.rem(w, 2)
    chip = lax.div(w, 2)
    twin = w + 1 - 2 * core
    chips = n_wide // 2
    for i in range(chips):
        for c in range(2):
            part[c, i, 0] = padded[i * 8:(i + 1) * 8, c * SLAB:(c + 1) * SLAB]
            tile, column = GRAM_TILES[2 * i + c]
            tile = tile + first_gram
            part[c, i, 1] = padded[tile * 8:(tile + 1) * 8, column * SLAB:(column + 1) * SLAB]

    to_twin = copy(part.at[1 - core], core_in, send_sem.at[6], core_sem.at[0], {"wide": twin})
    to_twin.start()
    to_twin.wait_recv()
    pair[...] = part[core] + core_in[...]

    around = sorted(((dx, dy) for dx in range(4) for dy in range(4) if dx or dy),
                    key=lambda at: -min(at[0], 4 - at[0]) - min(at[1], 4 - at[1]))

    def chip_at(dx, dy):
        return lax.rem(lax.div(chip, 4) + dx, 4) * 4 + lax.rem(lax.rem(chip, 4) + dy, 4)

    for dx, dy in around:
        to = chip_at(dx, dy)
        copy(pair.at[to], gather_in.at[chip], send_sem.at[3], red_sem, {"wide": 2 * to + core}).start()
    gather_in[chip] = pair[chip]
    parts_in = total_of(gather_in, send_sem.at[3], red_sem, chips - 1)
    parts_in.wait_recv()
    total[...] = jnp.sum(gather_in[...], axis=0)

    for dx, dy in around:
        to = chip_at(dx, dy)
        copy(total, gathered.at[core, chip], send_sem.at[4], all_sem, {"wide": 2 * to + core}).start()
    gathered[core, chip] = total[...]
    totals_in = total_of(gather_in, send_sem.at[4], all_sem, chips - 1)
    totals_in.wait_recv()
    all_to_twin = copy(gathered.at[core], gathered.at[core], send_sem.at[7], core_sem.at[1], {"wide": twin})
    all_to_twin.start()
    all_to_twin.wait_recv()

    solved = []
    for c in range(2):
        rows = [gathered[c, i, 0] for i in range(chips)]
        rows += [gathered[i % 2, i // 2, 1] for i in range(n_wide) if GRAM_TILES[i][1] == c]
        solved.append(dot_t(split(jnp.concatenate(rows, axis=0)), split(diag[c])))
    scaled = []
    for s in range(STEPS):
        c, at = s * BW // SLAB, s * BW % SLAB
        value = solved[c][:x_rows, at:at + BW]
        if s:
            overlap = solved[c][x_rows:x_rows + s * BW, at:at + BW]
            value = value - dot(split(jnp.concatenate(scaled, axis=1)), split(overlap))
        scaled.append(value)
    u = split(jnp.concatenate(scaled, axis=1))
    for held, first in sides:
        for m in range(0, half, 2):
            at = pl.multiple_of((first + m) * SLAB, 2 * SLAB)
            out_ref[:, pl.ds(at, 2 * SLAB)] = pair_x(first + m) - dot(u, split(pair_v(held, m)))

    total_of(own, send_sem.at[0], feed_sem.at[0], side).wait_send()
    flowed = flow.at[:, :, pl.ds(0, hops * PIECE)]
    copy(flowed, flowed, send_sem.at[1], feed_sem.at[0], {"row": near}).wait_send()
    for c, home, slot in ends:
        for m in range(half):
            distance, start, onward = fixed(c, home, m)
            pl.when(r == home)(start.wait_send)
            for wanted, move in onward:
                pl.when(wanted)(move.wait_send)
    other_x.wait_send()
    all_done.wait_send()
    parts_in.wait_send()
    totals_in.wait_send()
    to_twin.wait_send()
    all_to_twin.wait_send()


def body(n_row, n_wide, eigvec_t, householder, wy_factor, block_place, offsets):
    local = eigvec_t.shape[0]
    ncols = householder.shape[2]
    slabs = ncols // SLAB
    side = slabs * PIECE
    x = eigvec_t.reshape(local, n_wide, slabs, SLAB).transpose(1, 2, 0, 3)
    chips = n_wide // 2
    hbm = pl.BlockSpec(memory_space=pltpu.HBM)
    operands = [pltpu.with_memory_space_constraint(v, pltpu.HBM)
                for v in (block_place, offsets, x, householder, wy_factor)]
    f32 = jnp.float32
    return pl.pallas_call(
        functools.partial(kernel, n_row, n_wide),
        out_shape=jax.ShapeDtypeStruct((local * n_wide, ncols), f32),
        in_specs=[hbm] * 5,
        out_specs=pl.BlockSpec(memory_space=pltpu.VMEM),
        scratch_shapes=[
            pltpu.SMEM(block_place.shape, jnp.int32),
            pltpu.SMEM(offsets.shape, jnp.int32),
            pltpu.VMEM(householder.shape, f32),
            pltpu.VMEM(wy_factor.shape, f32),
            pltpu.VMEM((2, SLAB, SLAB), f32),
            pltpu.VMEM((2 * side, SLAB), f32),
            pltpu.VMEM((side, SLAB), f32),
            pltpu.VMEM((2, LINES, side, SLAB), f32),
            pltpu.VMEM((slabs // 2, STEPS, BW, SLAB), f32),
            pltpu.VMEM((slabs // 2, STEPS, BW, SLAB), f32),
            pltpu.VMEM((slabs, n_wide, local, SLAB), f32),
            pltpu.VMEM((2, chips, 2, 8, SLAB), f32),
            pltpu.VMEM((chips, 2, 8, SLAB), f32),
            pltpu.VMEM((chips, 2, 8, SLAB), f32),
            pltpu.VMEM((chips, 2, 8, SLAB), f32),
            pltpu.VMEM((2, 8, SLAB), f32),
            pltpu.VMEM((2, chips, 2, 8, SLAB), f32),
            pltpu.SemaphoreType.DMA((slabs * CUTS,)),
            pltpu.SemaphoreType.DMA((2, LINES, slabs * CUTS)),
            pltpu.SemaphoreType.DMA,
            pltpu.SemaphoreType.DMA((2, slabs // 2)),
            pltpu.SemaphoreType.DMA((2,)),
            pltpu.SemaphoreType.DMA,
            pltpu.SemaphoreType.DMA((2,)),
            pltpu.SemaphoreType.DMA,
            pltpu.SemaphoreType.DMA,
            pltpu.SemaphoreType.DMA((9,)),
            pltpu.SemaphoreType.DMA((5,)),
        ],
        compiler_params=pltpu.CompilerParams(collective_id=0, has_side_effects=True, vmem_limit_bytes=32 << 20),
    )(*operands)


def solution(mesh):
    n_row, n_wide = mesh.shape["row"], mesh.shape["wide"]
    return jax.shard_map(
        functools.partial(body, n_row, n_wide),
        mesh=mesh,
        in_specs=(P(("row", "wide"), None), P("row", None, "wide"), P(), P(), P()),
        out_specs=P("row", "wide"),
        check_vma=False,
    )
```

```python
import functools

import jax
import jax.numpy as jnp
from jax import lax
from jax.experimental import pallas as pl
from jax.experimental.pallas import tpu as pltpu
from jax.sharding import PartitionSpec as P

MESH = pl.DeviceIdType.MESH
STEPS, BW, SLAB, CUBE = 6, 32, 128, 4
FREE = STEPS - 2
CUTS = FREE // 2
LINES, LAG, GROUP = 2, 1, 2
PIECE = CUTS * BW
CHUNK = BW
GRAM_TILES = [(i, 0) for i in range(12)] + [(i, 1) for i in range(20)]


def split(a):
    high = a.astype(jnp.bfloat16)
    return high, (a - high.astype(jnp.float32)).astype(jnp.bfloat16)


def contract(a, b, dims):
    (a1, a2), (b1, b2) = a, b

    def one(x, y):
        return lax.dot_general(x, y, (dims, ((), ())), preferred_element_type=jnp.float32)

    return one(a1, b1) + (one(a1, b2) + one(a2, b1))


def dot_t(a, b):
    return contract(a, b, ((1,), (1,)))


def dot(a, b):
    return contract(a, b, ((1,), (0,)))


def kernel(n_row, n_wide, place_hbm, offset_hbm, x_ref, h_hbm, t_hbm, out_ref,
           place_ref, offset_ref, h_ref, t_ref, diag, own, feed, flow, mine_v, other_v, xs,
           part, core_in, pair, gather_in, total, gathered,
           feed_sem, flow_sem, done_sem, fixed_sem, fixed_done_sem, x_sem, core_sem, red_sem, all_sem, send_sem, local_sem):
    r = lax.axis_index("row")
    w = lax.axis_index("wide")
    slots = h_ref.shape[0]
    slabs = h_ref.shape[2] // SLAB
    pieces = slabs
    side = pieces * PIECE
    q = lax.rem(r, 2)
    a = lax.div(r, 2)
    mine, other = q * side, (1 - q) * side

    def row(delta):
        return lax.rem(r + delta + n_row, n_row)

    near, far = row(1 - 2 * q), row(2 * q - 1)

    barrier = pltpu.get_barrier_semaphore()
    for delta in (1, -1, 2, -2):
        pl.semaphore_signal(barrier, inc=1, device_id={"row": row(delta)}, device_id_type=MESH)

    def greet(d, carry):
        peer = lax.rem(w + d, n_wide)
        pl.semaphore_signal(barrier, inc=1, device_id={"wide": peer}, device_id_type=MESH)
        return carry

    load_h = pltpu.make_async_copy(h_hbm, h_ref, local_sem.at[0])
    load_t = pltpu.make_async_copy(t_hbm, t_ref, local_sem.at[1])
    load_x = pltpu.make_async_copy(x_ref.at[w], xs.at[:, w], local_sem.at[2])
    load_place = pltpu.make_async_copy(place_hbm, place_ref, local_sem.at[3])
    load_offset = pltpu.make_async_copy(offset_hbm, offset_ref, local_sem.at[4])
    load_place.start()
    load_offset.start()
    load_h.start()
    load_t.start()
    load_x.start()
    lax.fori_loop(1, n_wide, greet, 0)
    load_place.wait()
    load_offset.wait()
    load_h.wait()

    places = [place_ref[s] for s in range(STEPS)]
    channel, taken = [], 2
    for place in places:
        end = jnp.where(place == slots * n_row - 1, 1, taken)
        channel.append(jnp.where(place == 0, 0, end))
        taken = taken + jnp.where((place == 0) | (place == slots * n_row - 1), 0, 1)

    def of_channel(c, values):
        return sum(jnp.where(channel[s] == c, values[s], 0) for s in range(STEPS))

    starts = [offset_ref[s] for s in range(STEPS)]
    lane = lax.broadcasted_iota(jnp.int32, (BW, SLAB), 1) + w * (slabs * SLAB)
    ends = ((0, 0, 0), (1, n_row - 1, slots - 1))
    half = slabs // 2
    free = []
    for c in range(FREE):
        place = of_channel(2 + c, places)
        start = jnp.where(lax.div(place, slots) == r, of_channel(2 + c, starts), n_wide * slabs * SLAB)
        free.append((lax.rem(place, slots), start))

    def stage(first):
        for m in range(half):
            at = pl.multiple_of((first + m) * SLAB, SLAB)
            for c, (slot, start) in enumerate(free):
                block = h_ref[slot, :, pl.ds(at, SLAB)]
                own[pl.ds(((first + m) * FREE + c) * BW, BW)] = jnp.where(lane + at >= start, block, 0.0)

    stage((1 - q) * half)
    pl.semaphore_wait(barrier, n_wide + 3)

    def copy(src, dst, send, recv, to):
        return pltpu.make_async_remote_copy(
            src_ref=src, dst_ref=dst, send_sem=send, recv_sem=recv, device_id=to, device_id_type=MESH)

    def span(start, size):
        return pl.ds(pl.multiple_of(start, 8), size)

    def send_feed(t):
        for to, odd in ((near, 0), (far, 1)):
            i = lax.div(to, 2) - t + pieces
            i = i + lax.rem(i + odd, 2) * (1 + 2 * t)
            for line in range(LINES):
                for at, size, n in chunks_of(lax.rem(i + line * (pieces // LINES), pieces), isinstance(t, int) and t == 0):
                    copy(own.at[span(other + at, size)], feed.at[span(at, size)], send_sem.at[0], feed_sem.at[n],
                         {"row": to}).start()

    def chunks_of(i, single):
        return [(i * PIECE + j * CHUNK, CHUNK, i * CUTS + j) for j in range(CUTS)] if single else [(i * PIECE, PIECE, i * CUTS)]

    def send_x(d):
        peer = lax.rem(w + d, n_wide)
        copy(x_ref.at[peer], xs.at[:, w], send_sem.at[2], x_sem, {"wide": peer}).start()

    def hop(t, d, line, at, j):
        buf = flow.at[d, line, span(at, CHUNK)]
        return copy(buf, buf, send_sem.at[1], flow_sem.at[d, line, (t + 1) * CUTS + j], {"row": row(2 - 4 * d)})

    def piece(t, d, line):
        return lax.rem(a - t + d * (1 + 2 * t) + line * (pieces // LINES) + pieces, pieces)

    def send_finished(t, d, line):
        i = piece(t, d, line)
        to = near + lax.rem(i, 2) * (far - near)
        m = lax.div(i, 2)
        for j in range(CUTS):
            at, c = i * PIECE + j * CHUNK, 2 + lax.rem(i, 2) * CUTS + j
            here, flowed = span(mine + at, CHUNK), span(at, CHUNK)
            mine_v[m, c] = flow[0, line, flowed] + flow[1, line, flowed] - own[here]
            copy(mine_v.at[m, c], other_v.at[m, c], send_sem.at[5], done_sem, {"row": to}).start()

    def add_feed(t, d, line, single):
        for at, size, n in chunks_of(piece(t, d, line), single):
            here, fed = span(mine + at, size), span(at, size)
            copy(own.at[here], feed.at[fed], send_sem.at[0], feed_sem.at[n], {"row": near}).wait_recv()
            own[here] = own[here] + feed[fed]

    def advance(t, d, line, first=False, last=False):
        for j in range(CUTS):
            at = piece(t, d, line) * PIECE + j * CHUNK
            here, flowed = span(mine + at, CHUNK), span(at, CHUNK)
            if first:
                flow[d, line, flowed] = own[here]
            else:
                hop(t - 1, d, line, at, j).wait_recv()
                flow[d, line, flowed] = flow[d, line, flowed] + own[here]
            if not last:
                hop(t, d, line, at, j).start()

    def first_stream(t):
        crossed_right = lax.div(r + 2 * n_row, CUBE) - lax.div(r + 2 * n_row - 2 * t, CUBE)
        crossed_left = lax.div(r + 2 * t, CUBE) - lax.div(r, CUBE)
        return lax.div(crossed_right - crossed_left + 1, 2)

    def spread(t):
        share = n_wide * 2 // pieces
        lax.fori_loop(t * share, (t + 1) * share, lambda d, c: (send_x(d), c)[1], 0)

    def fixed(c, home, m):
        root = home // 2
        ahead, behind = lax.rem(a - root + pieces, pieces), lax.rem(root - a + pieces, pieces)
        held = mine_v.at[m, c]

        def to(row_at, source, target, sem):
            return copy(source.at[m, c], target.at[m, c], send_sem.at[8], sem, {"row": row_at})

        start = to(near, other_v, mine_v, fixed_sem.at[c, m])
        return jnp.minimum(ahead, behind), start, (
            (ahead < half, to(row(2), mine_v, mine_v, fixed_sem.at[c, m])),
            (behind < half - 1, to(row(-2), mine_v, mine_v, fixed_sem.at[c, m])),
            (near != home, to(near, mine_v, other_v, fixed_done_sem.at[c])))

    def start_fixed():
        for c, home, slot in ends:
            @pl.when(r == home)
            def _(c=c, home=home):
                for m in range(half):
                    fixed(c, home, m)[1].start()

    def pass_fixed(t):
        for c, home, slot in ends:
            root = home // 2
            distance = jnp.minimum(lax.rem(a - root + pieces, pieces), lax.rem(root - a + pieces, pieces))
            turn = t - LAG - distance

            @pl.when((turn >= 0) & (turn < half // GROUP))
            def _(c=c, home=home, turn=turn):
                for m in range(GROUP):
                    distance, start, onward = fixed(c, home, turn * GROUP + m)
                    pl.when(r != home)(start.wait_recv)
                    for wanted, move in onward:
                        pl.when(wanted)(move.start)

    def step(t, last=False):
        d = first_stream(t)
        for line in range(LINES):
            for way in (d, 1 - d):
                advance(t, way, line, last=last)

    feeds = half // LINES

    def feed_in(t, single):
        for d in range(2):
            for line in range(LINES):
                add_feed(t, d, line, single)

    def middle(t, carry):
        pl.when(t < feeds)(lambda: feed_in(t, False))
        step(t)
        pass_fixed(t)
        pl.when(t < feeds - 2)(lambda: send_feed(t + 2))
        spread(t)
        return carry

    send_feed(0)
    for c, home, slot in ends:
        @pl.when(r == home)
        def _(c=c, slot=slot):
            start = of_channel(c, starts)
            for m in range(half):
                for held, first in ((mine_v, q * half), (other_v, (1 - q) * half)):
                    at = pl.multiple_of((first + m) * SLAB, SLAB)
                    block = h_ref[slot, :, pl.ds(at, SLAB)]
                    held[m, c] = jnp.where(lane + at >= start, block, 0.0)
    start_fixed()
    send_feed(1)
    stage(q * half)
    for d in range(2):
        for line in range(LINES):
            add_feed(0, d, line, True)
            advance(0, d, line, first=True)
    if feeds > 2:
        send_feed(2)
    for d in range(1, n_wide * 2 // pieces):
        send_x(d)
    lax.fori_loop(1, half, middle, 0)
    hops = half + half // LINES - 1
    for t in range(half, hops + 1):
        if t == hops:
            first = first_stream(t)
            for line in range(LINES):
                for d in (first, 1 - first):
                    advance(t, d, line, last=True)
                    send_finished(t, d, line)
        else:
            step(t)
            for line in range(LINES):
                for d in range(2):
                    send_finished(t, d, line)
        pass_fixed(t)
    for t in range(hops + 1, half + half // GROUP + LAG):
        pass_fixed(t)

    def total_of(buf, send, recv, count):
        return copy(buf.at[pl.ds(0, count)], buf.at[pl.ds(0, count)], send, recv, {"row": near})

    load_t.wait()
    diag[...] = jnp.zeros_like(diag)
    for s in range(STEPS):
        at = s * BW % SLAB
        diag[s * BW // SLAB, at:at + BW, at:at + BW] = t_ref[s]
    load_x.wait()
    others = n_wide - 1
    other_x = copy(x_ref.at[pl.ds(0, others)], xs.at[:, pl.ds(0, others)], send_sem.at[2], x_sem, {"row": near})
    other_x.wait_recv()
    x_rows = xs.shape[1] * xs.shape[2]
    all_done = total_of(own, send_sem.at[5], done_sem, side)

    def pair_v(held, m):
        return jnp.concatenate(
            [jnp.concatenate([held[k, channel[s]] for s in range(STEPS)], axis=0) for k in (m, m + 1)], axis=1)

    def pair_x(k):
        return jnp.concatenate([xs[k].reshape(x_rows, SLAB), xs[k + 1].reshape(x_rows, SLAB)], axis=1)

    sides = ((mine_v, q * half), (other_v, (1 - q) * half))

    def products(held, first):
        acc = None
        for m in range(0, half, 2):
            v, x = pair_v(held, m), pair_x(first + m)
            v, x = split(v), split(x)
            product = dot_t([jnp.concatenate(both, axis=0) for both in zip(x, v)], v)
            acc = product if acc is None else acc + product
        return acc

    acc = products(*sides[0])
    all_done.wait_recv()
    for c, home, slot in ends:
        pl.when(r != home)(copy(mine_v.at[:, c], other_v.at[:, c], send_sem.at[8], fixed_done_sem.at[c],
                                {"row": near}).wait_recv)
    acc = acc + products(*sides[1])

    wide = 2 * SLAB
    padded = jnp.concatenate([acc, jnp.zeros((acc.shape[0], wide - acc.shape[1]), jnp.float32)], axis=1)
    first_gram = x_rows // 8
    core = lax.rem(w, 2)
    chip = lax.div(w, 2)
    twin = w + 1 - 2 * core
    chips = n_wide // 2
    for i in range(chips):
        for c in range(2):
            part[c, i, 0] = padded[i * 8:(i + 1) * 8, c * SLAB:(c + 1) * SLAB]
            tile, column = GRAM_TILES[2 * i + c]
            tile = tile + first_gram
            part[c, i, 1] = padded[tile * 8:(tile + 1) * 8, column * SLAB:(column + 1) * SLAB]

    to_twin = copy(part.at[1 - core], core_in, send_sem.at[6], core_sem.at[0], {"wide": twin})
    to_twin.start()
    to_twin.wait_recv()
    pair[...] = part[core] + core_in[...]

    around = sorted(((dx, dy) for dx in range(4) for dy in range(4) if dx or dy),
                    key=lambda at: -min(at[0], 4 - at[0]) - min(at[1], 4 - at[1]))

    def chip_at(dx, dy):
        return lax.rem(lax.div(chip, 4) + dx, 4) * 4 + lax.rem(lax.rem(chip, 4) + dy, 4)

    for dx, dy in around:
        to = chip_at(dx, dy)
        copy(pair.at[to], gather_in.at[chip], send_sem.at[3], red_sem, {"wide": 2 * to + core}).start()
    gather_in[chip] = pair[chip]
    parts_in = total_of(gather_in, send_sem.at[3], red_sem, chips - 1)
    parts_in.wait_recv()
    total[...] = jnp.sum(gather_in[...], axis=0)

    for dx, dy in around:
        to = chip_at(dx, dy)
        copy(total, gathered.at[core, chip], send_sem.at[4], all_sem, {"wide": 2 * to + core}).start()
    gathered[core, chip] = total[...]
    totals_in = total_of(gather_in, send_sem.at[4], all_sem, chips - 1)
    totals_in.wait_recv()
    all_to_twin = copy(gathered.at[core], gathered.at[core], send_sem.at[7], core_sem.at[1], {"wide": twin})
    all_to_twin.start()
    all_to_twin.wait_recv()

    solved = []
    for c in range(2):
        rows = [gathered[c, i, 0] for i in range(chips)]
        rows += [gathered[i % 2, i // 2, 1] for i in range(n_wide) if GRAM_TILES[i][1] == c]
        solved.append(dot_t(split(jnp.concatenate(rows, axis=0)), split(diag[c])))
    scaled = []
    for s in range(STEPS):
        c, at = s * BW // SLAB, s * BW % SLAB
        value = solved[c][:x_rows, at:at + BW]
        if s:
            overlap = solved[c][x_rows:x_rows + s * BW, at:at + BW]
            value = value - dot(split(jnp.concatenate(scaled, axis=1)), split(overlap))
        scaled.append(value)
    u = split(jnp.concatenate(scaled, axis=1))
    for held, first in sides:
        for m in range(0, half, 2):
            at = pl.multiple_of((first + m) * SLAB, 2 * SLAB)
            out_ref[:, pl.ds(at, 2 * SLAB)] = pair_x(first + m) - dot(u, split(pair_v(held, m)))

    total_of(own, send_sem.at[0], feed_sem.at[0], side).wait_send()
    flowed = flow.at[:, :, pl.ds(0, hops * PIECE)]
    copy(flowed, flowed, send_sem.at[1], feed_sem.at[0], {"row": near}).wait_send()
    for c, home, slot in ends:
        for m in range(half):
            distance, start, onward = fixed(c, home, m)
            pl.when(r == home)(start.wait_send)
            for wanted, move in onward:
                pl.when(wanted)(move.wait_send)
    other_x.wait_send()
    all_done.wait_send()
    parts_in.wait_send()
    totals_in.wait_send()
    to_twin.wait_send()
    all_to_twin.wait_send()


def body(n_row, n_wide, eigvec_t, householder, wy_factor, block_place, offsets):
    local = eigvec_t.shape[0]
    ncols = householder.shape[2]
    slabs = ncols // SLAB
    side = slabs * PIECE
    x = eigvec_t.reshape(local, n_wide, slabs, SLAB).transpose(1, 2, 0, 3)
    chips = n_wide // 2
    hbm = pl.BlockSpec(memory_space=pltpu.HBM)
    operands = [pltpu.with_memory_space_constraint(v, pltpu.HBM)
                for v in (block_place, offsets, x, householder, wy_factor)]
    f32 = jnp.float32
    return pl.pallas_call(
        functools.partial(kernel, n_row, n_wide),
        out_shape=jax.ShapeDtypeStruct((local * n_wide, ncols), f32),
        in_specs=[hbm] * 5,
        out_specs=pl.BlockSpec(memory_space=pltpu.VMEM),
        scratch_shapes=[
            pltpu.SMEM(block_place.shape, jnp.int32),
            pltpu.SMEM(offsets.shape, jnp.int32),
            pltpu.VMEM(householder.shape, f32),
            pltpu.VMEM(wy_factor.shape, f32),
            pltpu.VMEM((2, SLAB, SLAB), f32),
            pltpu.VMEM((2 * side, SLAB), f32),
            pltpu.VMEM((side, SLAB), f32),
            pltpu.VMEM((2, LINES, side, SLAB), f32),
            pltpu.VMEM((slabs // 2, STEPS, BW, SLAB), f32),
            pltpu.VMEM((slabs // 2, STEPS, BW, SLAB), f32),
            pltpu.VMEM((slabs, n_wide, local, SLAB), f32),
            pltpu.VMEM((2, chips, 2, 8, SLAB), f32),
            pltpu.VMEM((chips, 2, 8, SLAB), f32),
            pltpu.VMEM((chips, 2, 8, SLAB), f32),
            pltpu.VMEM((chips, 2, 8, SLAB), f32),
            pltpu.VMEM((2, 8, SLAB), f32),
            pltpu.VMEM((2, chips, 2, 8, SLAB), f32),
            pltpu.SemaphoreType.DMA((slabs * CUTS,)),
            pltpu.SemaphoreType.DMA((2, LINES, slabs * CUTS)),
            pltpu.SemaphoreType.DMA,
            pltpu.SemaphoreType.DMA((2, slabs // 2)),
            pltpu.SemaphoreType.DMA((2,)),
            pltpu.SemaphoreType.DMA,
            pltpu.SemaphoreType.DMA((2,)),
            pltpu.SemaphoreType.DMA,
            pltpu.SemaphoreType.DMA,
            pltpu.SemaphoreType.DMA((9,)),
            pltpu.SemaphoreType.DMA((5,)),
        ],
        compiler_params=pltpu.CompilerParams(collective_id=0, has_side_effects=True, vmem_limit_bytes=32 << 20),
    )(*operands)


def solution(mesh):
    n_row, n_wide = mesh.shape["row"], mesh.shape["wide"]
    return jax.shard_map(
        functools.partial(body, n_row, n_wide),
        mesh=mesh,
        in_specs=(P(("row", "wide"), None), P("row", None, "wide"), P(), P(), P()),
        out_specs=P("row", "wide"),
        check_vma=False,
    )
```
